512 devices in a mesh: box: 32 (over y_lo, z), dir: 16 (over y_hi, x, core).
Axes of the slice: x: 4, y: 4 (y_hi: 2, y_lo: 2; y = y_hi * 2 + y_lo), z: 16, core: 2. Of those that a mesh axis runs over, the one named last changes fastest.
Arguments:
- coarse_field: float32 [2048, 2, 4, 2048], P('box', None, None, 'dir'), may hold values from -6 to 6
- trans_table: float32 [316, 2, 2048], P(None, None, 'dir'), may hold values from -1.5 to 1.5
- partner_ids: int32 [2048, 30], P('box'), may hold values from 0 to 2047, as said below
- partner_types: int32 [2048, 30], P('box'), may hold values from 0 to 315
- partner_count: int32 [2048], P('box'), may hold values from 15 to 30
- child_count: int32 [2048], P('box'), may hold values from 1 to 7, as said below
- child_octant: int32 [8192], P('box'), may hold values from 0 to 7
- dir_angles: float32 [2, 2048], replicated, may hold values from -3.140625 to 3.140625
- stencil_ids: int32 [2048, 4], replicated, may hold values from 0 to 511, as said below
- stencil_weights: float32 [2048, 4], replicated, may hold values from -1.8 to 1.8
Outputs:
- fine_field: float32 [8192, 2, 4, 512], P(('box', 'dir'))
The draws below stay inside these ranges and needn't reach their ends.
Inputs may be any that keep to these rules, and one draw needn't show every extreme that they name: `partner_ids`: coarse box b sits on a grid whose z coordinate takes the two highest bits of b (the higher one as its bit 1) and whose x and y coordinates take the lower bits in turn (x from bit 0, y from bit 1, x from bit 2, and so on); the slots of b name distinct boxes that are children of neighbours of b's parent and not adjacent to b. `child_count`: each aligned block of 64 coarse boxes has exactly 256 children in all. stencil_ids[c, s] lies within 2 of c // 4, counted circularly over 512 directions.
All inputs are finite; a program needn't handle non-finite values.
Results may differ from the reference program's by a relative error of at most 0.0003.
Values sent between devices are 32-bit elements; how exact they have to be, the bound alone decides.
A program may use at most 64 MiB of HBM per device.

```python
import jax
import jax.numpy as jnp
from jax import lax

BC = 64
NS = 4
J = 30
NT = 316
KC = 2048
S = 4
KF = 512
NBC = 2048
NBF = 8192
N_BOX = 32


def bit_plan(total_bits):
    plan = []
    for position in range(total_bits):
        if position >= total_bits - 2:
            plan.append((2, position - (total_bits - 2)))
        else:
            plan.append((position % 2, position // 2))
    return plan


def morton_split(box_ids, total_bits):
    coordinates = [jnp.zeros_like(box_ids) for which in range(3)]
    for position, entry in enumerate(bit_plan(total_bits)):
        coordinates[entry[0]] = coordinates[entry[0]] + box_ids // 2 ** position % 2 * 2 ** entry[1]
    return coordinates


def morton_join(coordinates, total_bits):
    joined = jnp.zeros_like(coordinates[0])
    for position, entry in enumerate(bit_plan(total_bits)):
        joined = joined + coordinates[entry[0]] // 2 ** entry[1] % 2 * 2 ** position
    return joined


def draw_partner_ids(key, part):
    total_bits = NBC.bit_length() - 1
    plan = bit_plan(total_bits)
    extents = [2 ** len([entry for entry in plan if entry[0] == which]) for which in range(3)]
    box_ids = jnp.arange(NBC, dtype=jnp.int32)
    coordinates = morton_split(box_ids, total_bits)
    steps_six = jnp.arange(6, dtype=jnp.int32)
    offset_grid = [jnp.broadcast_to(steps_six[:, None, None], (6, 6, 6)).reshape(216), jnp.broadcast_to(steps_six[None, :, None], (6, 6, 6)).reshape(216), jnp.broadcast_to(steps_six[None, None, :], (6, 6, 6)).reshape(216)]
    candidates = []
    valid = jnp.ones((NBC, 216), dtype=bool)
    farthest = jnp.zeros((NBC, 216), jnp.int32)
    for which in range(3):
        offsets = offset_grid[which][None, :] - 2 - (coordinates[which] % 2)[:, None]
        placed = coordinates[which][:, None] + offsets
        valid = valid & (placed >= 0) & (placed < extents[which])
        farthest = jnp.maximum(farthest, jnp.abs(offsets))
        candidates.append(jnp.clip(placed, 0, extents[which] - 1))
    valid = valid & (farthest >= 2)
    cand_ids = morton_join(candidates, total_bits)
    scores = jax.random.randint(key, (NBC, 216), 0, 2 ** 20) * 256 + jnp.arange(216, dtype=jnp.int32)[None, :]
    scores = jnp.where(valid, scores, -1)
    unused, chosen = lax.top_k(scores, J)
    return jnp.take_along_axis(cand_ids, chosen, axis=1).astype(jnp.int32)


def draw_partner_count(key, part):
    counts = jax.random.randint(key, (NBC,), J // 2, J + 1)
    counts = counts.at[0].set(J).at[1].set(J // 2)
    return counts.astype(jnp.int32)


def draw_child_count(key, part):
    moved = jax.random.randint(key, (NBC // 2,), -3, 4)
    moved = moved.at[0].set(3)
    counts = jnp.stack([4 + moved, 4 - moved], axis=1).reshape(NBC)
    return counts.astype(jnp.int32)


def draw_stencil_ids(key, part):
    jitter = jax.random.randint(key, (KC, 2), 0, 2)
    centre = jnp.arange(KC, dtype=jnp.int32) // 4
    offsets = jnp.stack([jnp.full((KC,), -2, jnp.int32), jitter[:, 0] - 1, jitter[:, 1], jnp.full((KC,), 2, jnp.int32)], axis=1)
    return ((centre[:, None] + offsets) % KF).astype(jnp.int32)


def plant(array, rng, smallest, largest):
    longest = array.shape.index(max(array.shape))
    spots = []
    for shift in (0, 1):
        where = [jax.random.randint(jax.random.fold_in(rng, axis), (), 0, length) for axis, length in enumerate(array.shape)]
        where[longest] = (where[longest] + shift) % array.shape[longest]
        spots.append(tuple(where))
    return array.at[spots[0]].set(smallest).at[spots[1]].set(largest)


def level_of(stream_key, shape, cuts, low, high):
    level, own = 1.0, jax.random.fold_in(stream_key, 6)
    for dim, shards_of in cuts:
        draws = jnp.exp(jax.random.uniform(jax.random.fold_in(own, dim), (shards_of,), jnp.float32, low / len(cuts), high / len(cuts)))
        level = level * jnp.repeat(draws, shape[dim] // shards_of).reshape([-1 if axis == dim else 1 for axis in range(len(shape))])
    return level


def bell_draw(rng, dims, deviation, limit, shards=(), kind=jnp.bfloat16):
    loudness = level_of(rng, dims, shards, -0.22, 0.18) if shards else 1.0
    result = jax.random.normal(rng, dims, jnp.float32) * deviation * loudness
    return jnp.minimum(jnp.maximum(result, -limit), limit).astype(kind)


def setup_inputs(seed: int = 0) -> dict:
    streams_of = jax.random.split(jax.random.key(seed), 11)
    coarse_field = bell_draw(streams_of[0], (NBC, 2, NS, KC), 1.0, 6.0, ((0, 32), (3, 16)), jnp.float32)
    trans_table = bell_draw(streams_of[1], (NT, 2, KC), 0.25, 1.5, ((2, 16),), jnp.float32)
    partner_ids = draw_partner_ids(jax.random.fold_in(streams_of[10], 71), 0)
    partner_types = plant(jax.random.randint(streams_of[3], (NBC, J), 0, NT), jax.random.fold_in(streams_of[3], 1), 0, NT - 1).astype(jnp.int32)
    partner_count = draw_partner_count(jax.random.fold_in(streams_of[10], 71), 0)
    child_count = draw_child_count(jax.random.fold_in(streams_of[10], 71), 0)
    child_octant = plant(jax.random.randint(streams_of[6], (NBF,), 0, 8), jax.random.fold_in(streams_of[6], 1), 0, 7).astype(jnp.int32)
    dir_angles = jnp.clip(jax.random.uniform(streams_of[7], (2, KC), jnp.float32, -3.140625, 3.140625), -3.140625, 3.140625)
    stencil_ids = draw_stencil_ids(jax.random.fold_in(streams_of[10], 71), 0)
    stencil_weights = bell_draw(streams_of[9], (KC, S), 0.3, 1.8, (), jnp.float32)
    return dict(coarse_field=coarse_field, trans_table=trans_table, partner_ids=partner_ids, partner_types=partner_types, partner_count=partner_count, child_count=child_count, child_octant=child_octant, dir_angles=dir_angles, stencil_ids=stencil_ids, stencil_weights=stencil_weights)


wave_scale = 3.0


def reference(coarse_field, trans_table, partner_ids, partner_types, partner_count, child_count, child_octant, dir_angles, stencil_ids, stencil_weights):
    live_mask = (jnp.arange(J, dtype=jnp.int32)[None, :] < partner_count[:, None]).astype(jnp.float32)

    def translate(running, column):
        part_ids, type_ids, weight = column
        source = jnp.take(coarse_field, part_ids, axis=0)
        tab_row = jnp.take(trans_table, type_ids, axis=0)
        table_real = tab_row[:, 0, None, :] * weight[:, None, None]
        table_imag = tab_row[:, 1, None, :] * weight[:, None, None]
        real_part = table_real * source[:, 0] + table_imag * source[:, 1]
        imag_part = table_real * source[:, 1] - table_imag * source[:, 0]
        return running + jnp.stack([real_part, imag_part], axis=1), None

    zeros_init = jnp.zeros((NBC, 2, NS, KC), jnp.float32)
    translated, _ = lax.scan(translate, zeros_init, (partner_ids.T, partner_types.T, live_mask.T))

    bounds = jnp.cumsum(child_count).astype(jnp.int32)
    parent = jnp.searchsorted(bounds, jnp.arange(NBF, dtype=jnp.int32), side="right").astype(jnp.int32)

    theta_cols = dir_angles[0]
    phi_cols = dir_angles[1]
    unit_x = jnp.sin(theta_cols) * jnp.cos(phi_cols)
    unit_y = jnp.sin(theta_cols) * jnp.sin(phi_cols)
    unit_z = jnp.cos(theta_cols)

    matrix = jnp.zeros((KC, KF), jnp.float32)
    targets = jnp.arange(KF, dtype=jnp.int32)
    for point in range(S):
        matrix = matrix + jnp.where(stencil_ids[:, point, None] == targets[None, :], stencil_weights[:, point, None], 0.0)

    def level_block(pieces):
        parent_blk, octant_blk = pieces
        sign_x = 1.0 - 2.0 * (octant_blk % 2).astype(jnp.float32)
        sign_y = 1.0 - 2.0 * ((octant_blk // 2) % 2).astype(jnp.float32)
        sign_z = 1.0 - 2.0 * (octant_blk // 4).astype(jnp.float32)
        phase_angle = wave_scale * (sign_x[:, None] * unit_x[None, :] + sign_y[:, None] * unit_y[None, :] + sign_z[:, None] * unit_z[None, :])
        cosine = jnp.cos(phase_angle)[:, None, :]
        sine = jnp.sin(phase_angle)[:, None, :]
        gathered = jnp.take(translated, parent_blk, axis=0)
        real_part = gathered[:, 0] * cosine + gathered[:, 1] * sine
        imag_part = gathered[:, 1] * cosine - gathered[:, 0] * sine
        shifted = jnp.stack([real_part, imag_part], axis=1)
        return jnp.einsum("rtnc,cf->rtnf", shifted, matrix, precision=lax.Precision.HIGHEST)

    blocks = lax.map(level_block, (parent.reshape(N_BOX, 4 * BC), child_octant.reshape(N_BOX, 4 * BC)))
    return blocks.reshape(NBF, 2, NS, KF)
```

```python
import functools

import jax
import jax.numpy as jnp
from jax import lax
from jax.experimental import pallas as pl
from jax.experimental.pallas import tpu as pltpu
from jax.sharding import PartitionSpec as P

MESH = pl.DeviceIdType.MESH
wave_scale = 3.0

RING = 16
HOPS = 8
TILE = 64
QUAD = 16

REACH = (
    ((8, 0), (1, 8), (2, 8), (3, 8)),
    ((8, 1), (3, 8), (8, 7), (5, 8)),
    ((8, 2), (8, 7), (0, 8), (1, 8)),
    ((8, 3), (6, 8), (8, 1), (3, 8)),
    ((8, 3), (1, 8), (8, 6), (3, 8)),
    ((8, 1), (8, 0), (7, 8), (2, 8)),
    ((8, 5), (7, 8), (8, 3), (1, 8)),
    ((8, 3), (8, 2), (8, 1), (0, 8)),
)


def reach_code(way, origin):
    place = origin % 8
    code = jnp.int32(0)
    for which in range(8):
        packed = sum(REACH[which][quad][way] * 16**quad for quad in range(4))
        code = jnp.where(place == which, jnp.int32(packed), code)
    return code


def place_of(z):
    return z % 2 + 2 * (z // 4 % 2), z // 2 % 2


def z_of(dx, dy):
    return dx % 2 + 2 * dy + 4 * (dx // 2)


def lane_iota(rows=8):
    return lax.broadcasted_iota(jnp.int32, (rows, 128), 1)


def roll_lanes(value, shift):
    shift = shift % 128
    return pltpu.roll(value, shift, 1) if shift else value


def build_interp(me_dir, ids_ref, weights_ref, matrix_ref):
    relative = (ids_ref[...] - 32 * me_dir + 2 + 512) % 512
    weights = weights_ref[...]
    row = lax.broadcasted_iota(jnp.int32, (128, 128), 0)
    for sub in range(4):
        wanted = (row - 32 * ((sub + me_dir) % 4) + 2 + 128) % 128
        total = jnp.zeros((128, 128), jnp.float32)
        for point in range(4):
            hit = relative[point : point + 1, :] == wanted
            total = total + jnp.where(hit, weights[point : point + 1, :], 0.0)
        inner = (wanted >= 2) & (wanted < 34)
        columns = slice(128 * sub, 128 * sub + 128)
        matrix_ref[0:128, columns] = jnp.where(inner, total, 0.0)
        matrix_ref[128:256, columns] = jnp.where(inner, 0.0, total)


def pack_rows(shifted_ref, matrix_ref, send_ref, chunk):
    rows = shifted_ref[pl.ds(16 * chunk, 16)].reshape(128, 512)
    product = lax.dot_general(
        rows,
        matrix_ref[...],
        (((1,), (1,)), ((), ())),
        precision=lax.Precision.HIGHEST,
        preferred_element_type=jnp.float32,
    )
    for owner in range(4):
        edges = None
        for line in range(4):
            at = 32 * owner + 8 * line
            send_ref[4 * chunk + owner, line] = product[at : at + 8, 0:128]
            piece = roll_lanes(product[at : at + 8, 128:256], 4 * line)
            edges = piece if edges is None else edges + piece
        send_ref[4 * chunk + owner, 4] = edges


def assemble(got_ref, out_ref):
    lane = lane_iota()
    group = lane // 32
    near = (lane + 2) % 32 < 4
    for sub in range(4):
        moved = (lane - 32 * sub + 128) % 128
        left_from = (moved + 2) // 32 % 4
        right_from = (moved + 96) // 32 % 4
        take_left = moved % 4 >= 2
        for quarter in range(4):
            left = right = None
            for source in range(4):
                left_at = 4 * quarter + source if source else 4 * ((quarter + 1) % 4)
                right_at = 4 * quarter + source if source < 3 else (4 * quarter + 15) % 16
                left_one, right_one = got_ref[left_at, 4], got_ref[right_at, 4]
                left = left_one if left is None else jnp.where(left_from == source, left_one, left)
                right = (
                    right_one if right is None else jnp.where(right_from == source, right_one, right)
                )
            edges = jnp.where(take_left, left, right)
            for line in range(4):
                main = None
                for at in range(4):
                    one = got_ref[4 * quarter + (at - sub) % 4, line]
                    main = one if main is None else jnp.where(group == at, one, main)
                main = roll_lanes(main, -32 * sub)
                extra = roll_lanes(edges, -(32 * sub + 4 * line))
                value = main + jnp.where(near, extra, 0.0)
                columns = slice(128 * quarter, 128 * quarter + 128)
                out_ref[4 * sub + line, 0, :, columns] = value[0:4]
                out_ref[4 * sub + line, 1, :, columns] = value[4:8]


def broadcast_table(raw_ref, table_ref, type_count):
    def step(tile, carry):
        rows = raw_ref[pl.ds(8 * tile, 8), :]
        for which in range(4):
            for part in range(2):
                at = 2 * which + part
                table_ref[4 * tile + which, part] = jnp.broadcast_to(rows[at : at + 1], (8, 128))
        return carry

    lax.fori_loop(0, type_count // 4, step, 0)
    table_ref[type_count] = jnp.zeros((2, 8, 128), jnp.float32)


def stage_indices(own, type_count, ids_ref, types_ref, count_ref, child_ref, octant_ref, stage_ref):
    slots = ids_ref.shape[0]
    slot = lax.broadcasted_iota(jnp.int32, (slots, TILE), 0)
    box = lax.broadcasted_iota(jnp.int32, (slots, TILE), 1)
    live = slot < count_ref[...]
    stage_ref[0:slots, 0:TILE] = jnp.where(live, ids_ref[...], own + box)
    stage_ref[32 : 32 + slots, 0:TILE] = jnp.where(live, types_ref[...], type_count)
    upto = lax.broadcasted_iota(jnp.int32, (TILE, TILE), 0)
    which = lax.broadcasted_iota(jnp.int32, (TILE, TILE), 1)
    bounds = jnp.sum(jnp.where(which <= upto, child_ref[...], 0), axis=1, keepdims=True)
    for half in range(2):
        fine = lax.broadcasted_iota(jnp.int32, (TILE, 128), 1) + 128 * half
        parent = jnp.sum(jnp.where(bounds <= fine, 1, 0), axis=0, keepdims=True)
        stage_ref[64 + half : 65 + half, :] = jnp.minimum(parent, TILE - 1)
    stage_ref[66:68, :] = octant_ref[...]


def build_phases(angle_ref, phase_ref):
    theta, phi = angle_ref[0:1, :], angle_ref[1:2, :]
    unit_x = jnp.sin(theta) * jnp.cos(phi)
    unit_y = jnp.sin(theta) * jnp.sin(phi)
    unit_z = jnp.cos(theta)
    octant = lax.broadcasted_iota(jnp.int32, (8, 128), 0)
    sign_x = 1.0 - 2.0 * (octant % 2).astype(jnp.float32)
    sign_y = 1.0 - 2.0 * (octant // 2 % 2).astype(jnp.float32)
    sign_z = 1.0 - 2.0 * (octant // 4).astype(jnp.float32)
    angle = wave_scale * (sign_x * unit_x + sign_y * unit_y + sign_z * unit_z)
    cosine, sine = jnp.cos(angle), jnp.sin(angle)
    for which in range(8):
        phase_ref[which, 0] = jnp.broadcast_to(cosine[which : which + 1], (8, 128))
        spread = jnp.broadcast_to(sine[which : which + 1], (8, 128))
        phase_ref[which, 1] = jnp.where(octant < 4, spread, -spread)


def translate_boxes(slots, index_ref, field_ref, table_ref, moved_ref):
    real_row = lax.broadcasted_iota(jnp.int32, (8, 128), 0) < 4

    def step(box, carry):
        sums = [None] * 4
        for slot in range(slots):
            source = field_ref[index_ref[slot, box] & (field_ref.shape[0] - 1)]
            kind = index_ref[32 + slot, box] & (table_ref.shape[0] - 1)
            for part in range(2):
                term = table_ref[kind, part] * source
                at = 2 * (slot % 2) + part
                sums[at] = term if sums[at] is None else sums[at] + term
        straight = sums[0] if sums[2] is None else sums[0] + sums[2]
        crossed = sums[1] if sums[3] is None else sums[1] + sums[3]
        crossed = pltpu.roll(crossed, 4, 0)
        value = straight + jnp.where(real_row, crossed, -crossed)
        moved_ref[box, 0] = value
        moved_ref[box, 1] = pltpu.roll(value, 4, 0)
        return carry

    lax.fori_loop(0, TILE, step, 0)


def shift_children(index_ref, moved_ref, phase_ref, shifted_ref):
    def step(owner, carry):
        for fine in range(16):
            sub, line = fine // 4, fine % 4
            at = 16 * owner + fine
            parent = index_ref[64 + at // 128, at % 128] & (TILE - 1)
            octant = index_ref[66 + at // 128, at % 128] & 7
            value = (
                moved_ref[parent, 0] * phase_ref[octant, 0]
                + moved_ref[parent, 1] * phase_ref[octant, 1]
            )
            shifted_ref[4 * owner + line, :, 128 * sub : 128 * sub + 128] = value
        return carry

    lax.fori_loop(0, 16, step, 0)


def kernel(
    type_count,
    x_hbm,
    table_hbm,
    ids_hbm,
    types_hbm,
    count_hbm,
    child_hbm,
    octant_hbm,
    angles_hbm,
    stencil_hbm,
    weights_hbm,
    out_ref,
    field,
    raw,
    table,
    ids,
    types,
    count,
    child,
    octant,
    angles,
    stencil,
    weights,
    stage,
    index,
    phase,
    moved,
    shifted,
    matrix,
    outbox,
    inbox,
    load_sem,
    stage_sem,
    ring_send,
    ring_recv,
    side_send,
    side_recv,
    swap_send,
    swap_recv,
):
    me_box, me_dir = lax.axis_index("box"), lax.axis_index("dir")
    z, plane = me_box % RING, me_box // RING
    dx, dy = place_of(z)
    own = TILE * me_box
    slots = ids_hbm.shape[0]
    up, down = (z + 1) % RING, (z + RING - 1) % RING

    here = pl.ds(pl.multiple_of(128 * me_dir, 128), 128)
    loads = [
        pltpu.make_async_copy(src, dst, load_sem.at[at])
        for at, (src, dst) in enumerate(
            (
                (x_hbm, field.at[pl.ds(own, TILE)]),
                (table_hbm, raw),
                (ids_hbm, ids),
                (types_hbm, types),
                (count_hbm, count),
                (child_hbm, child),
                (octant_hbm, octant),
                (angles_hbm.at[:, here], angles),
                (stencil_hbm.at[:, here], stencil),
                (weights_hbm.at[:, here], weights),
            )
        )
    ]
    for load in loads:
        load.start()

    barrier = pltpu.get_barrier_semaphore()
    for place in (up, down):
        pl.semaphore_signal(
            barrier, inc=1, device_id={"box": RING * plane + place}, device_id_type=MESH
        )
    pl.semaphore_signal(
        barrier, inc=1, device_id={"box": RING * (1 - plane) + z}, device_id_type=MESH
    )
    for step in range(1, 16):
        pl.semaphore_signal(
            barrier, inc=1, device_id={"dir": (me_dir + step) % 16}, device_id_type=MESH
        )
    pl.semaphore_wait(barrier, 18)

    def rows_of(which_plane, origin, start, size):
        return field.at[pl.ds(TILE * (RING * which_plane + origin) + start, size)]

    def hop(way, step, quad, origin, first=False):
        rows = rows_of(plane, origin, QUAD * quad, QUAD)
        return pltpu.make_async_remote_copy(
            src_ref=x_hbm.at[pl.ds(QUAD * quad, QUAD)] if first else rows,
            dst_ref=rows,
            send_sem=ring_send.at[way, step, quad],
            recv_sem=ring_recv.at[way, step, quad],
            device_id={"box": RING * plane + (down if way else up)},
            device_id_type=MESH,
        )

    def side(which_plane, origin, start, size, quad, part, first=False):
        rows = rows_of(which_plane, origin, start, size)
        return pltpu.make_async_remote_copy(
            src_ref=x_hbm.at[pl.ds(start, size)] if first else rows,
            dst_ref=rows,
            send_sem=side_send.at[origin, quad, part],
            recv_sem=side_recv.at[origin, quad, part],
            device_id={"box": RING * (1 - plane) + z},
            device_id_type=MESH,
        )

    for quad in (0, 3, 1, 2):
        for way in range(2):
            far = reach_code(way, z) // 16**quad % 16

            @pl.when(far > 0)
            def _():
                hop(way, 0, quad, z, True).start()

    for quad in range(4):
        side(plane, z, QUAD * quad, QUAD, quad, 0, True).start()

    for load in loads:
        load.wait()
    stage_indices(own, type_count, ids, types, count, child, octant, stage)
    to_index = pltpu.make_async_copy(stage, index, stage_sem)
    to_index.start()
    build_interp(me_dir, stencil, weights, matrix)
    build_phases(angles, phase)
    broadcast_table(raw, table, type_count)
    to_index.wait()

    def ring_step(step, carry):
        for way in range(2):
            origin = (z + step) % RING if way else (z + RING - step) % RING
            code = reach_code(way, origin)
            from_x, from_y = place_of(origin)
            for quad in range(4):
                far = code // 16**quad % 16
                half_x, half_y = quad % 2, quad // 2
                same_x, same_y = from_x == dx, from_y == dy
                next_x = from_x - dx == 1 - 2 * half_x
                next_y = from_y - dy == 1 - 2 * half_y
                start = QUAD * quad

                @pl.when(step <= far)
                def _():
                    hop(way, step - 1, quad, origin).wait_recv()

                    @pl.when(step < far)
                    def _():
                        hop(way, step, quad, origin).start()

                    @pl.when(same_x & same_y)
                    def _():
                        side(plane, origin, start, 16, quad, 0).start()

                    @pl.when(same_x & next_y)
                    def _():
                        side(plane, origin, start + 8 * half_y, 8, quad, 0).start()

                    @pl.when(next_x & same_y)
                    def _():
                        side(plane, origin, start + 4 * half_x, 4, quad, 0).start()
                        side(plane, origin, start + 8 + 4 * half_x, 4, quad, 1).start()

                    @pl.when(next_x & next_y)
                    def _():
                        at = start + 4 * half_x + 8 * half_y
                        side(plane, origin, at, 4, quad, 0).start()

        return carry

    lax.fori_loop(1, HOPS + 1, ring_step, 0)

    def every_side(act, which_plane):
        for half in range(2):
            base = (z // 8 + half) % 2 * 8
            for quad in range(4):
                act(side(which_plane, base + z % 8, QUAD * quad, QUAD, quad, 0))
            across = base + z_of(dx, 1 - dy)
            for half_x in range(2):
                quad = half_x + 2 * dy
                act(side(which_plane, across, QUAD * quad + 8 * dy, 8, quad, 0))
            for half_x in range(2):
                to_x = dx + 1 - 2 * half_x

                @pl.when((to_x >= 0) & (to_x <= 3))
                def _():
                    beside = base + z_of(to_x, dy)
                    for half_y in range(2):
                        quad = half_x + 2 * half_y
                        start = QUAD * quad + 4 * half_x
                        act(side(which_plane, beside, start, 4, quad, 0))
                        act(side(which_plane, beside, start + 8, 4, quad, 1))
                    quad = half_x + 2 * dy
                    start = QUAD * quad + 4 * half_x + 8 * dy
                    act(side(which_plane, base + z_of(to_x, 1 - dy), start, 4, quad, 0))

    every_side(lambda copy: copy.wait_recv(), 1 - plane)

    translate_boxes(slots, index, field, table, moved)
    shift_children(index, moved, phase, shifted)

    def pack(chunk, carry):
        pack_rows(shifted, matrix, outbox, chunk)
        return carry

    lax.fori_loop(0, 4, pack, 0)

    def swap(to, source):
        return pltpu.make_async_remote_copy(
            src_ref=outbox.at[to],
            dst_ref=inbox.at[source],
            send_sem=swap_send.at[to],
            recv_sem=swap_recv.at[source],
            device_id={"dir": to},
            device_id_type=MESH,
        )

    def send(step, carry):
        swap((me_dir + step) % 16, me_dir).start()
        return carry

    lax.fori_loop(1, 16, send, 0)
    inbox[me_dir] = outbox[me_dir]

    every_side(lambda copy: copy.wait_send(), plane)

    def ring_drain(step, carry):
        for way in range(2):
            origin = (z + step) % RING if way else (z + RING - step) % RING
            code = reach_code(way, origin)
            for quad in range(4):

                @pl.when(step < code // 16**quad % 16)
                def _():
                    hop(way, step, quad, origin).wait_send()

        return carry

    lax.fori_loop(0, HOPS, ring_drain, 0)

    def receive(step, carry):
        other = (me_dir + step) % 16
        swap(other, other).wait_recv()
        swap(other, me_dir).wait_send()
        return carry

    lax.fori_loop(1, 16, receive, 0)
    assemble(inbox, out_ref)


def per_device(
    coarse_field,
    trans_table,
    partner_ids,
    partner_types,
    partner_count,
    child_count,
    child_octant,
    dir_angles,
    stencil_ids,
    stencil_weights,
):
    type_count = trans_table.shape[0]
    slots = partner_ids.shape[1]
    f32, i32 = jnp.float32, jnp.int32
    vmem, dma = pltpu.VMEM, pltpu.SemaphoreType.DMA
    return pl.pallas_call(
        functools.partial(kernel, type_count),
        out_shape=jax.ShapeDtypeStruct((16, 2, 4, 512), f32),
        in_specs=[pl.BlockSpec(memory_space=pl.ANY)] * 10,
        out_specs=pl.BlockSpec(memory_space=pltpu.VMEM),
        scratch_shapes=[
            vmem((2048, 8, 128), f32),
            vmem((2 * type_count, 128), f32),
            vmem((512, 2, 8, 128), f32),
            vmem((slots, TILE), i32),
            vmem((slots, TILE), i32),
            vmem((1, TILE), i32),
            vmem((1, TILE), i32),
            vmem((2, 128), i32),
            vmem((2, 128), f32),
            vmem((4, 128), i32),
            vmem((4, 128), f32),
            vmem((72, 128), i32),
            pltpu.SMEM((72, 128), i32),
            vmem((8, 2, 8, 128), f32),
            vmem((TILE, 2, 8, 128), f32),
            vmem((64, 8, 512), f32),
            vmem((256, 512), f32),
            vmem((16, 5, 8, 128), f32),
            vmem((16, 5, 8, 128), f32),
            dma((10,)),
            dma,
            dma((2, HOPS + 1, 4)),
            dma((2, HOPS + 1, 4)),
            dma((RING, 4, 2)),
            dma((RING, 4, 2)),
            dma((16,)),
            dma((16,)),
        ],
        compiler_params=pltpu.CompilerParams(collective_id=0, has_side_effects=True),
    )(
        coarse_field.reshape(TILE, 8, 128),
        trans_table.reshape(2 * type_count, 128),
        partner_ids.T,
        partner_types.T,
        partner_count.reshape(1, TILE),
        child_count.reshape(1, TILE),
        child_octant.reshape(2, 128),
        dir_angles,
        stencil_ids.T,
        stencil_weights.T,
    )


def solution(mesh):
    placed = (
        P("box", None, None, "dir"),
        P(None, None, "dir"),
        P("box", None),
        P("box", None),
        P("box"),
        P("box"),
        P("box"),
        P(),
        P(),
        P(),
    )
    return jax.shard_map(
        per_device,
        mesh=mesh,
        in_specs=placed,
        out_specs=P(("box", "dir"), None, None, None),
        check_vma=False,
    )
```

```python
import functools

import jax
import jax.numpy as jnp
from jax import lax
from jax.experimental import pallas as pl
from jax.experimental.pallas import tpu as pltpu
from jax.sharding import PartitionSpec as P

MESH = pl.DeviceIdType.MESH
wave_scale = 3.0

RING = 16
HOPS = 8
TILE = 64
QUAD = 16

REACH = (
    ((8, 0), (1, 8), (2, 8), (3, 8)),
    ((8, 1), (3, 8), (8, 7), (5, 8)),
    ((8, 2), (8, 7), (0, 8), (1, 8)),
    ((8, 3), (6, 8), (8, 1), (3, 8)),
    ((8, 3), (1, 8), (8, 6), (3, 8)),
    ((8, 1), (8, 0), (7, 8), (2, 8)),
    ((8, 5), (7, 8), (8, 3), (1, 8)),
    ((8, 3), (8, 2), (8, 1), (0, 8)),
)


def reach_code(way, origin):
    place = origin % 8
    code = jnp.int32(0)
    for which in range(8):
        packed = sum(REACH[which][quad][way] * 16**quad for quad in range(4))
        code = jnp.where(place == which, jnp.int32(packed), code)
    return code


def place_of(z):
    return z % 2 + 2 * (z // 4 % 2), z // 2 % 2


def z_of(dx, dy):
    return dx % 2 + 2 * dy + 4 * (dx // 2)


def lane_iota(rows=8):
    return lax.broadcasted_iota(jnp.int32, (rows, 128), 1)


def roll_lanes(value, shift):
    shift = shift % 128
    return pltpu.roll(value, shift, 1) if shift else value


def build_interp(me_dir, ids_ref, weights_ref, matrix_ref):
    relative = (ids_ref[...] - 32 * me_dir + 2 + 512) % 512
    weights = weights_ref[...]
    row = lax.broadcasted_iota(jnp.int32, (128, 128), 0)
    for sub in range(4):
        wanted = (row - 32 * ((sub + me_dir) % 4) + 2 + 128) % 128
        total = jnp.zeros((128, 128), jnp.float32)
        for point in range(4):
            hit = relative[point : point + 1, :] == wanted
            total = total + jnp.where(hit, weights[point : point + 1, :], 0.0)
        inner = (wanted >= 2) & (wanted < 34)
        columns = slice(128 * sub, 128 * sub + 128)
        matrix_ref[0:128, columns] = jnp.where(inner, total, 0.0)
        matrix_ref[128:256, columns] = jnp.where(inner, 0.0, total)


def pack_rows(shifted_ref, matrix_ref, send_ref, chunk):
    rows = shifted_ref[...].reshape(128, 512)
    product = lax.dot_general(
        rows,
        matrix_ref[...],
        (((1,), (1,)), ((), ())),
        precision=lax.Precision.HIGHEST,
        preferred_element_type=jnp.float32,
    )
    for owner in range(4):
        edges = None
        for line in range(4):
            at = 32 * owner + 8 * line
            send_ref[4 * chunk + owner, line] = product[at : at + 8, 0:128]
            piece = roll_lanes(product[at : at + 8, 128:256], 4 * line)
            edges = piece if edges is None else edges + piece
        send_ref[4 * chunk + owner, 4] = edges


def assemble(got_ref, out_ref):
    lane = lane_iota()
    group = lane // 32
    near = (lane + 2) % 32 < 4
    for sub in range(4):
        moved = (lane - 32 * sub + 128) % 128
        left_from = (moved + 2) // 32 % 4
        right_from = (moved + 96) // 32 % 4
        take_left = moved % 4 >= 2
        for quarter in range(4):
            left = right = None
            for source in range(4):
                left_at = 4 * quarter + source if source else 4 * ((quarter + 1) % 4)
                right_at = 4 * quarter + source if source < 3 else (4 * quarter + 15) % 16
                left_one, right_one = got_ref[left_at, 4], got_ref[right_at, 4]
                left = left_one if left is None else jnp.where(left_from == source, left_one, left)
                right = (
                    right_one if right is None else jnp.where(right_from == source, right_one, right)
                )
            edges = jnp.where(take_left, left, right)
            for line in range(4):
                main = None
                for at in range(4):
                    one = got_ref[4 * quarter + (at - sub) % 4, line]
                    main = one if main is None else jnp.where(group == at, one, main)
                main = roll_lanes(main, -32 * sub)
                extra = roll_lanes(edges, -(32 * sub + 4 * line))
                value = main + jnp.where(near, extra, 0.0)
                columns = slice(128 * quarter, 128 * quarter + 128)
                out_ref[4 * sub + line, 0, :, columns] = value[0:4]
                out_ref[4 * sub + line, 1, :, columns] = value[4:8]


def broadcast_table(raw_ref, table_ref, type_count):
    def step(tile, carry):
        rows = raw_ref[pl.ds(8 * tile, 8), :]
        for at in range(8):
            row = jnp.broadcast_to(rows[at : at + 1], (8, 128))
            table_ref[4 * tile + at // 2, at % 2] = row
        return carry

    lax.fori_loop(0, type_count // 4, step, 0)
    table_ref[type_count] = jnp.zeros((2, 8, 128), jnp.float32)


def stage_indices(own, type_count, ids_ref, types_ref, count_ref, child_ref, octant_ref, stage_ref):
    slots = ids_ref.shape[0]
    slot = lax.broadcasted_iota(jnp.int32, (slots, TILE), 0)
    box = lax.broadcasted_iota(jnp.int32, (slots, TILE), 1)
    live = slot < count_ref[...]
    source = jnp.where(live, ids_ref[...], own + box)
    kind = jnp.where(live, types_ref[...], type_count)
    stage_ref[0:slots, 0:TILE] = source * 65536 + kind
    upto = lax.broadcasted_iota(jnp.int32, (TILE, TILE), 0)
    which = lax.broadcasted_iota(jnp.int32, (TILE, TILE), 1)
    bounds = jnp.sum(jnp.where(which <= upto, child_ref[...], 0), axis=1, keepdims=True)
    for half in range(2):
        fine = lax.broadcasted_iota(jnp.int32, (TILE, 128), 1) + 128 * half
        parent = jnp.sum(jnp.where(bounds <= fine, 1, 0), axis=0, keepdims=True)
        parent = jnp.minimum(parent, TILE - 1)
        stage_ref[32 + half : 33 + half, :] = parent * 16 + octant_ref[half : half + 1, :]


def build_phases(angle_ref, phase_ref):
    theta, phi = angle_ref[0:1, :], angle_ref[1:2, :]
    unit_x = jnp.sin(theta) * jnp.cos(phi)
    unit_y = jnp.sin(theta) * jnp.sin(phi)
    unit_z = jnp.cos(theta)
    octant = lax.broadcasted_iota(jnp.int32, (8, 128), 0)
    sign_x = 1.0 - 2.0 * (octant % 2).astype(jnp.float32)
    sign_y = 1.0 - 2.0 * (octant // 2 % 2).astype(jnp.float32)
    sign_z = 1.0 - 2.0 * (octant // 4).astype(jnp.float32)
    angle = wave_scale * (sign_x * unit_x + sign_y * unit_y + sign_z * unit_z)
    cosine, sine = jnp.cos(angle), jnp.sin(angle)
    for which in range(8):
        phase_ref[which, 0] = jnp.broadcast_to(cosine[which : which + 1], (8, 128))
        spread = jnp.broadcast_to(sine[which : which + 1], (8, 128))
        phase_ref[which, 1] = jnp.where(octant < 4, spread, -spread)


def translate_boxes(slots, index_ref, field_ref, table_ref, moved_ref):
    real_row = lax.broadcasted_iota(jnp.int32, (8, 128), 0) < 4

    def step(box, carry):
        sums = [None] * 4
        for slot in range(slots):
            packed = index_ref[slot, box]
            source = field_ref[(packed >> 16) & (field_ref.shape[0] - 1)]
            kind = packed & (table_ref.shape[0] - 1)
            for part in range(2):
                term = table_ref[kind, part] * source
                at = 2 * (slot % 2) + part
                sums[at] = term if sums[at] is None else sums[at] + term
        straight = sums[0] if sums[2] is None else sums[0] + sums[2]
        crossed = sums[1] if sums[3] is None else sums[1] + sums[3]
        crossed = pltpu.roll(crossed, 4, 0)
        value = straight + jnp.where(real_row, crossed, -crossed)
        moved_ref[box, 0] = value
        moved_ref[box, 1] = pltpu.roll(value, 4, 0)
        return carry

    lax.fori_loop(0, TILE, step, 0, unroll=2)


def shift_children(chunk, index_ref, moved_ref, phase_ref, shifted_ref):
    for owner in range(4):
        for fine in range(16):
            sub, line = fine // 4, fine % 4
            at = 16 * owner + fine
            packed = index_ref[32 + chunk // 2, 64 * (chunk % 2) + at]
            parent, octant = (packed >> 4) & (TILE - 1), packed & 7
            value = (
                moved_ref[parent, 0] * phase_ref[octant, 0]
                + moved_ref[parent, 1] * phase_ref[octant, 1]
            )
            shifted_ref[4 * owner + line, :, 128 * sub : 128 * sub + 128] = value


def kernel(
    type_count,
    x_hbm,
    table_hbm,
    ids_hbm,
    types_hbm,
    count_hbm,
    child_hbm,
    octant_hbm,
    angles_hbm,
    stencil_hbm,
    weights_hbm,
    out_ref,
    field,
    raw,
    table,
    ids,
    types,
    count,
    child,
    octant,
    angles,
    stencil,
    weights,
    stage,
    index,
    phase,
    moved,
    shifted,
    matrix,
    outbox,
    inbox,
    load_sem,
    stage_sem,
    ring_send,
    ring_recv,
    side_send,
    side_recv,
    swap_send,
    swap_recv,
):
    me_box, me_dir = lax.axis_index("box"), lax.axis_index("dir")
    z, plane = me_box % RING, me_box // RING
    dx, dy = place_of(z)
    own = TILE * me_box
    slots = ids_hbm.shape[0]
    up, down = (z + 1) % RING, (z + RING - 1) % RING

    here = pl.ds(pl.multiple_of(128 * me_dir, 128), 128)
    loads = [
        pltpu.make_async_copy(src, dst, load_sem.at[at])
        for at, (src, dst) in enumerate(
            (
                (x_hbm, field.at[pl.ds(own, TILE)]),
                (table_hbm, raw),
                (ids_hbm, ids),
                (types_hbm, types),
                (count_hbm, count),
                (child_hbm, child),
                (octant_hbm, octant),
                (angles_hbm.at[:, here], angles),
                (stencil_hbm.at[:, here], stencil),
                (weights_hbm.at[:, here], weights),
            )
        )
    ]
    for load in loads:
        load.start()

    barrier = pltpu.get_barrier_semaphore()
    for place in (up, down):
        pl.semaphore_signal(
            barrier, inc=1, device_id={"box": RING * plane + place}, device_id_type=MESH
        )
    pl.semaphore_signal(
        barrier, inc=1, device_id={"box": RING * (1 - plane) + z}, device_id_type=MESH
    )
    for step in range(1, 16):
        pl.semaphore_signal(
            barrier, inc=1, device_id={"dir": (me_dir + step) % 16}, device_id_type=MESH
        )
    pl.semaphore_wait(barrier, 18)

    def rows_of(which_plane, origin, start, size):
        return field.at[pl.ds(TILE * (RING * which_plane + origin) + start, size)]

    def hop(way, step, quad, origin, first=False):
        rows = rows_of(plane, origin, QUAD * quad, QUAD)
        return pltpu.make_async_remote_copy(
            src_ref=x_hbm.at[pl.ds(QUAD * quad, QUAD)] if first else rows,
            dst_ref=rows,
            send_sem=ring_send.at[way, step, quad],
            recv_sem=ring_recv.at[way, step, quad],
            device_id={"box": RING * plane + (down if way else up)},
            device_id_type=MESH,
        )

    def side(which_plane, origin, start, size, quad, part, first=False):
        rows = rows_of(which_plane, origin, start, size)
        return pltpu.make_async_remote_copy(
            src_ref=x_hbm.at[pl.ds(start, size)] if first else rows,
            dst_ref=rows,
            send_sem=side_send.at[origin, quad, part],
            recv_sem=side_recv.at[origin, quad, part],
            device_id={"box": RING * (1 - plane) + z},
            device_id_type=MESH,
        )

    for quad in (0, 3, 1, 2):
        for way in range(2):
            far = reach_code(way, z) // 16**quad % 16

            @pl.when(far > 0)
            def _():
                hop(way, 0, quad, z, True).start()

    for quad in range(4):
        side(plane, z, QUAD * quad, QUAD, quad, 0, True).start()

    for load in loads:
        load.wait()
    stage_indices(own, type_count, ids, types, count, child, octant, stage)
    to_index = pltpu.make_async_copy(stage, index, stage_sem)
    to_index.start()
    build_interp(me_dir, stencil, weights, matrix)
    build_phases(angles, phase)
    broadcast_table(raw, table, type_count)
    to_index.wait()

    def ring_step(step, carry):
        for way in range(2):
            origin = (z + step) % RING if way else (z + RING - step) % RING
            code = reach_code(way, origin)
            from_x, from_y = place_of(origin)
            for quad in range(4):
                far = code // 16**quad % 16
                half_x, half_y = quad % 2, quad // 2
                same_x, same_y = from_x == dx, from_y == dy
                next_x = from_x - dx == 1 - 2 * half_x
                next_y = from_y - dy == 1 - 2 * half_y
                start = QUAD * quad

                @pl.when(step <= far)
                def _():
                    hop(way, step - 1, quad, origin).wait_recv()

                    @pl.when(step < far)
                    def _():
                        hop(way, step, quad, origin).start()

                    @pl.when(same_x & same_y)
                    def _():
                        side(plane, origin, start, 16, quad, 0).start()

                    @pl.when(same_x & next_y)
                    def _():
                        side(plane, origin, start + 8 * half_y, 8, quad, 0).start()

                    @pl.when(next_x & same_y)
                    def _():
                        side(plane, origin, start + 4 * half_x, 4, quad, 0).start()
                        side(plane, origin, start + 8 + 4 * half_x, 4, quad, 1).start()

                    @pl.when(next_x & next_y)
                    def _():
                        at = start + 4 * half_x + 8 * half_y
                        side(plane, origin, at, 4, quad, 0).start()

        return carry

    lax.fori_loop(1, HOPS + 1, ring_step, 0)

    def every_side(act, which_plane):
        for half in range(2):
            base = (z // 8 + half) % 2 * 8
            for quad in range(4):
                act(side(which_plane, base + z % 8, QUAD * quad, QUAD, quad, 0))
            across = base + z_of(dx, 1 - dy)
            for half_x in range(2):
                quad = half_x + 2 * dy
                act(side(which_plane, across, QUAD * quad + 8 * dy, 8, quad, 0))
            for half_x in range(2):
                to_x = dx + 1 - 2 * half_x

                @pl.when((to_x >= 0) & (to_x <= 3))
                def _():
                    beside = base + z_of(to_x, dy)
                    for half_y in range(2):
                        quad = half_x + 2 * half_y
                        start = QUAD * quad + 4 * half_x
                        act(side(which_plane, beside, start, 4, quad, 0))
                        act(side(which_plane, beside, start + 8, 4, quad, 1))
                    quad = half_x + 2 * dy
                    start = QUAD * quad + 4 * half_x + 8 * dy
                    act(side(which_plane, base + z_of(to_x, 1 - dy), start, 4, quad, 0))

    every_side(lambda copy: copy.wait_recv(), 1 - plane)

    translate_boxes(slots, index, field, table, moved)
    def swap(to, source):
        return pltpu.make_async_remote_copy(
            src_ref=outbox.at[to],
            dst_ref=inbox.at[source],
            send_sem=swap_send.at[to],
            recv_sem=swap_recv.at[source],
            device_id={"dir": to},
            device_id_type=MESH,
        )

    def pack(step, carry):
        chunk = (me_dir // 4 + 1 + step) % 4
        shift_children(chunk, index, moved, phase, shifted)
        pack_rows(shifted, matrix, outbox, chunk)
        for owner in range(4):
            to = 4 * chunk + owner

            @pl.when(to != me_dir)
            def _():
                swap(to, me_dir).start()

        return carry

    lax.fori_loop(0, 4, pack, 0)
    inbox[me_dir] = outbox[me_dir]

    every_side(lambda copy: copy.wait_send(), plane)

    def ring_drain(step, carry):
        for way in range(2):
            origin = (z + step) % RING if way else (z + RING - step) % RING
            code = reach_code(way, origin)
            for quad in range(4):

                @pl.when(step < code // 16**quad % 16)
                def _():
                    hop(way, step, quad, origin).wait_send()

        return carry

    lax.fori_loop(0, HOPS, ring_drain, 0)

    def receive(step, carry):
        other = (me_dir + step) % 16
        swap(other, other).wait_recv()
        swap(other, me_dir).wait_send()
        return carry

    lax.fori_loop(1, 16, receive, 0)
    assemble(inbox, out_ref)


def per_device(
    coarse_field,
    trans_table,
    partner_ids,
    partner_types,
    partner_count,
    child_count,
    child_octant,
    dir_angles,
    stencil_ids,
    stencil_weights,
):
    type_count = trans_table.shape[0]
    slots = partner_ids.shape[1]
    f32, i32 = jnp.float32, jnp.int32
    vmem, dma = pltpu.VMEM, pltpu.SemaphoreType.DMA
    return pl.pallas_call(
        functools.partial(kernel, type_count),
        out_shape=jax.ShapeDtypeStruct((16, 2, 4, 512), f32),
        in_specs=[pl.BlockSpec(memory_space=pl.ANY)] * 10,
        out_specs=pl.BlockSpec(memory_space=pltpu.VMEM),
        scratch_shapes=[
            vmem((2048, 8, 128), f32),
            vmem((2 * type_count, 128), f32),
            vmem((512, 2, 8, 128), f32),
            vmem((slots, TILE), i32),
            vmem((slots, TILE), i32),
            vmem((1, TILE), i32),
            vmem((1, TILE), i32),
            vmem((2, 128), i32),
            vmem((2, 128), f32),
            vmem((4, 128), i32),
            vmem((4, 128), f32),
            vmem((40, 128), i32),
            pltpu.SMEM((40, 128), i32),
            vmem((8, 2, 8, 128), f32),
            vmem((TILE, 2, 8, 128), f32),
            vmem((16, 8, 512), f32),
            vmem((256, 512), f32),
            vmem((16, 5, 8, 128), f32),
            vmem((16, 5, 8, 128), f32),
            dma((10,)),
            dma,
            dma((2, HOPS + 1, 4)),
            dma((2, HOPS + 1, 4)),
            dma((RING, 4, 2)),
            dma((RING, 4, 2)),
            dma((16,)),
            dma((16,)),
        ],
        compiler_params=pltpu.CompilerParams(collective_id=0, has_side_effects=True),
    )(
        coarse_field.reshape(TILE, 8, 128),
        trans_table.reshape(2 * type_count, 128),
        partner_ids.T,
        partner_types.T,
        partner_count.reshape(1, TILE),
        child_count.reshape(1, TILE),
        child_octant.reshape(2, 128),
        dir_angles,
        stencil_ids.T,
        stencil_weights.T,
    )


def solution(mesh):
    placed = (
        P("box", None, None, "dir"),
        P(None, None, "dir"),
        P("box", None),
        P("box", None),
        P("box"),
        P("box"),
        P("box"),
        P(),
        P(),
        P(),
    )
    return jax.shard_map(
        per_device,
        mesh=mesh,
        in_specs=placed,
        out_specs=P(("box", "dir"), None, None, None),
        check_vma=False,
    )
```

```python
import functools

import jax
import jax.numpy as jnp
from jax import lax
from jax.experimental import pallas as pl
from jax.experimental.pallas import tpu as pltpu
from jax.sharding import PartitionSpec as P

MESH = pl.DeviceIdType.MESH
wave_scale = 3.0

RING = 16
HOPS = 8
TILE = 64
PART = 8
PARTS = 8

REACH = (
    ((8, 0), (8, 0), (1, 8), (1, 8), (8, 0), (2, 8), (1, 8), (3, 8)),
    ((8, 1), (8, 1), (3, 8), (3, 8), (8, 1), (8, 7), (3, 8), (8, 6)),
    ((8, 2), (8, 0), (8, 7), (1, 8), (8, 0), (0, 8), (1, 8), (1, 8)),
    ((8, 3), (8, 1), (6, 8), (3, 8), (8, 1), (8, 1), (8, 5), (3, 8)),
    ((8, 3), (8, 3), (1, 8), (1, 8), (8, 3), (8, 6), (1, 8), (3, 8)),
    ((8, 1), (8, 1), (0, 8), (0, 8), (8, 1), (8, 7), (0, 8), (2, 8)),
    ((6, 8), (8, 3), (8, 7), (1, 8), (8, 3), (8, 3), (1, 8), (1, 8)),
    ((8, 3), (8, 1), (8, 2), (0, 8), (8, 1), (8, 1), (0, 8), (0, 8)),
)

ORDER = (
    (5, 0),
    (3, 1),
    (4, 0),
    (0, 1),
    (0, 0),
    (7, 1),
    (7, 0),
    (6, 0),
    (1, 1),
    (4, 1),
    (2, 0),
    (6, 1),
    (3, 0),
    (1, 0),
    (5, 1),
    (2, 1),
)


def reach_codes(way, origin):
    place = origin % 8
    codes = []
    for base in (0, 4):
        code = jnp.int32(0)
        for which in range(8):
            packed = sum(REACH[which][base + at][way] * 16**at for at in range(4))
            code = jnp.where(place == which, jnp.int32(packed), code)
        codes.append(code)
    return codes


def reach_of(codes, part):
    return codes[part // 4] // 16 ** (part % 4) % 16


def place_of(z):
    return z % 2 + 2 * (z // 4 % 2), z // 2 % 2


def z_of(dx, dy):
    return dx % 2 + 2 * dy + 4 * (dx // 2)


def lane_iota(rows=8):
    return lax.broadcasted_iota(jnp.int32, (rows, 128), 1)


def roll_lanes(value, shift):
    shift = shift % 128
    return pltpu.roll(value, shift, 1) if shift else value


def build_interp(me_dir, ids_ref, weights_ref, matrix_ref):
    relative = (ids_ref[...] - 32 * me_dir + 2 + 512) % 512
    weights = weights_ref[...]
    row = lax.broadcasted_iota(jnp.int32, (128, 128), 0)
    for sub in range(4):
        wanted = (row - 32 * ((sub + me_dir) % 4) + 2 + 128) % 128
        total = jnp.zeros((128, 128), jnp.float32)
        for point in range(4):
            hit = relative[point : point + 1, :] == wanted
            total = total + jnp.where(hit, weights[point : point + 1, :], 0.0)
        inner = (wanted >= 2) & (wanted < 34)
        columns = slice(128 * sub, 128 * sub + 128)
        matrix_ref[0:128, columns] = jnp.where(inner, total, 0.0)
        matrix_ref[128:256, columns] = jnp.where(inner, 0.0, total)


def pack_rows(shifted_ref, matrix_ref, send_ref, chunk):
    rows = shifted_ref[...].reshape(128, 512)
    product = lax.dot_general(
        rows,
        matrix_ref[...],
        (((1,), (1,)), ((), ())),
        precision=lax.Precision.HIGHEST,
        preferred_element_type=jnp.float32,
    )
    for owner in range(4):
        edges = None
        for line in range(4):
            at = 32 * owner + 8 * line
            send_ref[4 * chunk + owner, line] = product[at : at + 8, 0:128]
            piece = roll_lanes(product[at : at + 8, 128:256], 4 * line)
            edges = piece if edges is None else edges + piece
        send_ref[4 * chunk + owner, 4] = edges


def assemble(got_ref, out_ref):
    lane = lane_iota()
    group = lane // 32
    near = (lane + 2) % 32 < 4
    for sub in range(4):
        moved = (lane - 32 * sub + 128) % 128
        left_from = (moved + 2) // 32 % 4
        right_from = (moved + 96) // 32 % 4
        take_left = moved % 4 >= 2
        for quarter in range(4):
            left = right = None
            for source in range(4):
                left_at = 4 * quarter + source if source else 4 * ((quarter + 1) % 4)
                right_at = 4 * quarter + source if source < 3 else (4 * quarter + 15) % 16
                left_one, right_one = got_ref[left_at, 4], got_ref[right_at, 4]
                left = left_one if left is None else jnp.where(left_from == source, left_one, left)
                right = (
                    right_one if right is None else jnp.where(right_from == source, right_one, right)
                )
            edges = jnp.where(take_left, left, right)
            for line in range(4):
                main = None
                for at in range(4):
                    one = got_ref[4 * quarter + (at - sub) % 4, line]
                    main = one if main is None else jnp.where(group == at, one, main)
                main = roll_lanes(main, -32 * sub)
                extra = roll_lanes(edges, -(32 * sub + 4 * line))
                value = main + jnp.where(near, extra, 0.0)
                columns = slice(128 * quarter, 128 * quarter + 128)
                out_ref[4 * sub + line, 0, :, columns] = value[0:4]
                out_ref[4 * sub + line, 1, :, columns] = value[4:8]


def broadcast_table(raw_ref, table_ref, type_count):
    def step(tile, carry):
        rows = raw_ref[pl.ds(8 * tile, 8), :]
        for at in range(8):
            row = jnp.broadcast_to(rows[at : at + 1], (8, 128))
            table_ref[4 * tile + at // 2, at % 2] = row
        return carry

    lax.fori_loop(0, type_count // 4, step, 0)
    table_ref[type_count] = jnp.zeros((2, 8, 128), jnp.float32)


def stage_indices(
    own, type_count, ids_ref, types_ref, count_ref, child_ref, octant_ref, work_ref, stage_ref
):
    slots = ids_ref.shape[0]
    slot = lax.broadcasted_iota(jnp.int32, (slots, TILE), 0)
    box = lax.broadcasted_iota(jnp.int32, (slots, TILE), 1)
    live = slot < count_ref[...]
    work_ref[...] = jnp.zeros((128, 128), jnp.int32)
    work_ref[0:slots, 0:TILE] = jnp.where(live, ids_ref[...], own + box)
    work_ref[32 : 32 + slots, 0:TILE] = jnp.where(live, types_ref[...], type_count)
    stage_ref[0:TILE, :] = work_ref[...].T[0:TILE]
    upto = lax.broadcasted_iota(jnp.int32, (TILE, TILE), 0)
    which = lax.broadcasted_iota(jnp.int32, (TILE, TILE), 1)
    bounds = jnp.sum(jnp.where(which <= upto, child_ref[...], 0), axis=1, keepdims=True)
    for half in range(2):
        fine = lax.broadcasted_iota(jnp.int32, (TILE, 128), 1) + 128 * half
        parent = jnp.sum(jnp.where(bounds <= fine, 1, 0), axis=0, keepdims=True)
        parent = jnp.minimum(parent, TILE - 1)
        words = jnp.broadcast_to(parent * 16 + octant_ref[half : half + 1, :], (8, 128))
        at = TILE + 2 * half
        stage_ref[at : at + 1, :] = words[0:1]
        stage_ref[at + 1 : at + 2, :] = pltpu.roll(words, 64, 1)[0:1]


def build_phases(angle_ref, phase_ref):
    theta, phi = angle_ref[0:1, :], angle_ref[1:2, :]
    unit_x = jnp.sin(theta) * jnp.cos(phi)
    unit_y = jnp.sin(theta) * jnp.sin(phi)
    unit_z = jnp.cos(theta)
    octant = lax.broadcasted_iota(jnp.int32, (8, 128), 0)
    sign_x = 1.0 - 2.0 * (octant % 2).astype(jnp.float32)
    sign_y = 1.0 - 2.0 * (octant // 2 % 2).astype(jnp.float32)
    sign_z = 1.0 - 2.0 * (octant // 4).astype(jnp.float32)
    angle = wave_scale * (sign_x * unit_x + sign_y * unit_y + sign_z * unit_z)
    cosine, sine = jnp.cos(angle), jnp.sin(angle)
    for which in range(8):
        phase_ref[which, 0] = jnp.broadcast_to(cosine[which : which + 1], (8, 128))
        spread = jnp.broadcast_to(sine[which : which + 1], (8, 128))
        phase_ref[which, 1] = jnp.where(octant < 4, spread, -spread)


def translate_boxes(slots, index_ref, field_ref, table_ref, moved_ref):
    real_row = lax.broadcasted_iota(jnp.int32, (8, 128), 0) < 4

    def step(box, carry):
        sums = [None] * 4
        for slot in range(slots):
            source = field_ref[index_ref[box, slot]]
            kind = index_ref[box, 32 + slot]
            for part in range(2):
                term = table_ref[kind, part] * source
                at = 2 * (slot % 2) + part
                sums[at] = term if sums[at] is None else sums[at] + term
        straight = sums[0] if sums[2] is None else sums[0] + sums[2]
        crossed = sums[1] if sums[3] is None else sums[1] + sums[3]
        crossed = pltpu.roll(crossed, 4, 0)
        value = straight + jnp.where(real_row, crossed, -crossed)
        moved_ref[box, 0] = value
        moved_ref[box, 1] = pltpu.roll(value, 4, 0)
        return carry

    lax.fori_loop(0, TILE, step, 0)


def shift_children(chunk, index_ref, moved_ref, phase_ref, shifted_ref):
    for owner in range(4):
        for fine in range(16):
            sub, line = fine // 4, fine % 4
            at = 16 * owner + fine
            packed = index_ref[TILE + chunk, at]
            parent, octant = (packed >> 4) & (TILE - 1), packed & 7
            value = (
                moved_ref[parent, 0] * phase_ref[octant, 0]
                + moved_ref[parent, 1] * phase_ref[octant, 1]
            )
            shifted_ref[4 * owner + line, :, 128 * sub : 128 * sub + 128] = value


def kernel(
    type_count,
    x_hbm,
    table_hbm,
    ids_hbm,
    types_hbm,
    count_hbm,
    child_hbm,
    octant_hbm,
    angles_hbm,
    stencil_hbm,
    weights_hbm,
    out_ref,
    field,
    raw,
    table,
    ids,
    types,
    count,
    child,
    octant,
    angles,
    stencil,
    weights,
    work,
    stage,
    index,
    phase,
    moved,
    shifted,
    matrix,
    outbox,
    inbox,
    load_sem,
    stage_sem,
    ring_send,
    ring_recv,
    side_send,
    side_recv,
    swap_send,
    swap_recv,
):
    me_box, me_dir = lax.axis_index("box"), lax.axis_index("dir")
    z, plane = me_box % RING, me_box // RING
    dx, dy = place_of(z)
    own = TILE * me_box
    slots = ids_hbm.shape[0]
    up, down = (z + 1) % RING, (z + RING - 1) % RING

    here = pl.ds(pl.multiple_of(128 * me_dir, 128), 128)
    loads = [
        pltpu.make_async_copy(src, dst, load_sem.at[at])
        for at, (src, dst) in enumerate(
            (
                (x_hbm, field.at[pl.ds(own, TILE)]),
                (table_hbm, raw),
                (ids_hbm, ids),
                (types_hbm, types),
                (count_hbm, count),
                (child_hbm, child),
                (octant_hbm, octant),
                (angles_hbm.at[:, here], angles),
                (stencil_hbm.at[:, here], stencil),
                (weights_hbm.at[:, here], weights),
            )
        )
    ]
    for load in loads:
        load.start()

    barrier = pltpu.get_barrier_semaphore()
    for place in (up, down):
        pl.semaphore_signal(
            barrier, inc=1, device_id={"box": RING * plane + place}, device_id_type=MESH
        )
    pl.semaphore_signal(
        barrier, inc=1, device_id={"box": RING * (1 - plane) + z}, device_id_type=MESH
    )
    for step in range(1, 16):
        pl.semaphore_signal(
            barrier, inc=1, device_id={"dir": (me_dir + step) % 16}, device_id_type=MESH
        )
    pl.semaphore_wait(barrier, 18)

    def rows_of(which_plane, origin, start, size):
        return field.at[pl.ds(TILE * (RING * which_plane + origin) + start, size)]

    def hop(way, step, part, origin, first=False):
        rows = rows_of(plane, origin, PART * part, PART)
        return pltpu.make_async_remote_copy(
            src_ref=x_hbm.at[pl.ds(PART * part, PART)] if first else rows,
            dst_ref=rows,
            send_sem=ring_send.at[way, step, part],
            recv_sem=ring_recv.at[way, step, part],
            device_id={"box": RING * plane + (down if way else up)},
            device_id_type=MESH,
        )

    def side(which_plane, origin, part, shift, size, first=False):
        start = PART * part + shift
        rows = rows_of(which_plane, origin, start, size)
        return pltpu.make_async_remote_copy(
            src_ref=x_hbm.at[pl.ds(start, size)] if first else rows,
            dst_ref=rows,
            send_sem=side_send.at[origin, part],
            recv_sem=side_recv.at[origin, part],
            device_id={"box": RING * (1 - plane) + z},
            device_id_type=MESH,
        )

    first_codes = [reach_codes(way, z) for way in range(2)]
    for part, way in ORDER:

        @pl.when(reach_of(first_codes[way], part) > 0)
        def _():
            hop(way, 0, part, z, True).start()

    for part in range(PARTS):
        side(plane, z, part, 0, PART, True).start()

    for load in loads:
        load.wait()
    stage_indices(own, type_count, ids, types, count, child, octant, work, stage)
    to_index = pltpu.make_async_copy(stage, index, stage_sem)
    to_index.start()
    build_interp(me_dir, stencil, weights, matrix)
    build_phases(angles, phase)
    broadcast_table(raw, table, type_count)
    to_index.wait()

    def ring_step(step, carry):
        origins = [(z + RING - step) % RING, (z + step) % RING]
        codes = [reach_codes(way, origins[way]) for way in range(2)]
        spots = [place_of(origin) for origin in origins]
        for part, way in ORDER:
            origin, (from_x, from_y) = origins[way], spots[way]
            far = reach_of(codes[way], part)
            half_x, line = part // 2 % 2, part // 4 * 2 + part % 2
            near_y = from_y == dy
            if line == 0:
                near_y = near_y | (from_y > dy)
            if line == 3:
                near_y = near_y | (from_y < dy)

            @pl.when(step <= far)
            def _():
                hop(way, step - 1, part, origin).wait_recv()

                @pl.when(step < far)
                def _():
                    hop(way, step, part, origin).start()

                @pl.when(near_y & (from_x == dx))
                def _():
                    side(plane, origin, part, 0, PART).start()

                @pl.when(near_y & (from_x - dx == 1 - 2 * half_x))
                def _():
                    side(plane, origin, part, 4 * half_x, 4).start()

        return carry

    lax.fori_loop(1, HOPS + 1, ring_step, 0)

    def every_side(act, which_plane):
        for half in range(2):
            base = (z // 8 + half) % 2 * 8
            across = base + z_of(dx, 1 - dy)
            for part in range(PARTS):
                act(side(which_plane, base + z % 8, part, 0, PART))
            for half_x in range(2):
                act(side(which_plane, across, 5 * dy + 2 * half_x, 0, PART))
            for half_x in range(2):
                to_x = dx + 1 - 2 * half_x

                @pl.when((to_x >= 0) & (to_x <= 3))
                def _():
                    for line in range(4):
                        part = line // 2 * 4 + line % 2 + 2 * half_x
                        act(side(which_plane, base + z_of(to_x, dy), part, 4 * half_x, 4))
                    part = 5 * dy + 2 * half_x
                    act(side(which_plane, base + z_of(to_x, 1 - dy), part, 4 * half_x, 4))

    every_side(lambda copy: copy.wait_recv(), 1 - plane)

    translate_boxes(slots, index, field, table, moved)
    def swap(to, source):
        return pltpu.make_async_remote_copy(
            src_ref=outbox.at[to],
            dst_ref=inbox.at[source],
            send_sem=swap_send.at[to],
            recv_sem=swap_recv.at[source],
            device_id={"dir": to},
            device_id_type=MESH,
        )

    def pack(step, carry):
        chunk = (me_dir // 4 + 1 + step) % 4
        shift_children(chunk, index, moved, phase, shifted)
        pack_rows(shifted, matrix, outbox, chunk)
        for owner in range(4):
            to = 4 * chunk + owner

            @pl.when(to != me_dir)
            def _():
                swap(to, me_dir).start()

        return carry

    lax.fori_loop(0, 4, pack, 0)
    inbox[me_dir] = outbox[me_dir]

    every_side(lambda copy: copy.wait_send(), plane)

    def ring_drain(step, carry):
        for way in range(2):
            origin = (z + step) % RING if way else (z + RING - step) % RING
            codes = reach_codes(way, origin)
            for part in range(PARTS):

                @pl.when(step < reach_of(codes, part))
                def _():
                    hop(way, step, part, origin).wait_send()

        return carry

    lax.fori_loop(0, HOPS, ring_drain, 0)

    def receive(step, carry):
        other = (me_dir + step) % 16
        swap(other, other).wait_recv()
        swap(other, me_dir).wait_send()
        return carry

    lax.fori_loop(1, 16, receive, 0)
    assemble(inbox, out_ref)


def per_device(
    coarse_field,
    trans_table,
    partner_ids,
    partner_types,
    partner_count,
    child_count,
    child_octant,
    dir_angles,
    stencil_ids,
    stencil_weights,
):
    type_count = trans_table.shape[0]
    slots = partner_ids.shape[1]
    f32, i32 = jnp.float32, jnp.int32
    vmem, dma = pltpu.VMEM, pltpu.SemaphoreType.DMA
    return pl.pallas_call(
        functools.partial(kernel, type_count),
        out_shape=jax.ShapeDtypeStruct((16, 2, 4, 512), f32),
        in_specs=[pl.BlockSpec(memory_space=pl.ANY)] * 10,
        out_specs=pl.BlockSpec(memory_space=pltpu.VMEM),
        scratch_shapes=[
            vmem((2048, 8, 128), f32),
            vmem((2 * type_count, 128), f32),
            vmem((512, 2, 8, 128), f32),
            vmem((slots, TILE), i32),
            vmem((slots, TILE), i32),
            vmem((1, TILE), i32),
            vmem((1, TILE), i32),
            vmem((2, 128), i32),
            vmem((2, 128), f32),
            vmem((4, 128), i32),
            vmem((4, 128), f32),
            vmem((128, 128), i32),
            vmem((72, 128), i32),
            pltpu.SMEM((72, 128), i32),
            vmem((8, 2, 8, 128), f32),
            vmem((TILE, 2, 8, 128), f32),
            vmem((16, 8, 512), f32),
            vmem((256, 512), f32),
            vmem((16, 5, 8, 128), f32),
            vmem((16, 5, 8, 128), f32),
            dma((10,)),
            dma,
            dma((2, HOPS + 1, PARTS)),
            dma((2, HOPS + 1, PARTS)),
            dma((RING, PARTS)),
            dma((RING, PARTS)),
            dma((16,)),
            dma((16,)),
        ],
        compiler_params=pltpu.CompilerParams(collective_id=0, has_side_effects=True),
    )(
        coarse_field.reshape(TILE, 8, 128),
        trans_table.reshape(2 * type_count, 128),
        partner_ids.T,
        partner_types.T,
        partner_count.reshape(1, TILE),
        child_count.reshape(1, TILE),
        child_octant.reshape(2, 128),
        dir_angles,
        stencil_ids.T,
        stencil_weights.T,
    )


def solution(mesh):
    placed = (
        P("box", None, None, "dir"),
        P(None, None, "dir"),
        P("box", None),
        P("box", None),
        P("box"),
        P("box"),
        P("box"),
        P(),
        P(),
        P(),
    )
    return jax.shard_map(
        per_device,
        mesh=mesh,
        in_specs=placed,
        out_specs=P(("box", "dir"), None, None, None),
        check_vma=False,
    )
```

```python
import functools

import jax
import jax.numpy as jnp
from jax import lax
from jax.experimental import pallas as pl
from jax.experimental.pallas import tpu as pltpu
from jax.sharding import PartitionSpec as P

MESH = pl.DeviceIdType.MESH
wave_scale = 3.0

RING = 16
HOPS = 8
TILE = 64
PART = 8
PARTS = 8

REACH = (
    ((8, 0), (8, 0), (1, 8), (1, 8), (8, 0), (2, 8), (1, 8), (3, 8)),
    ((8, 1), (8, 1), (3, 8), (3, 8), (8, 1), (8, 7), (3, 8), (8, 6)),
    ((8, 2), (8, 0), (8, 7), (1, 8), (8, 0), (0, 8), (1, 8), (1, 8)),
    ((8, 3), (8, 1), (6, 8), (3, 8), (8, 1), (8, 1), (8, 5), (3, 8)),
    ((8, 3), (8, 3), (1, 8), (1, 8), (8, 3), (8, 6), (1, 8), (3, 8)),
    ((8, 1), (8, 1), (0, 8), (0, 8), (8, 1), (8, 7), (0, 8), (2, 8)),
    ((6, 8), (8, 3), (8, 7), (1, 8), (8, 3), (8, 3), (1, 8), (1, 8)),
    ((8, 3), (8, 1), (8, 2), (0, 8), (8, 1), (8, 1), (0, 8), (0, 8)),
)

ORDER = (
    (5, 0),
    (3, 1),
    (4, 0),
    (0, 1),
    (0, 0),
    (7, 1),
    (7, 0),
    (6, 0),
    (1, 1),
    (4, 1),
    (2, 0),
    (6, 1),
    (3, 0),
    (1, 0),
    (5, 1),
    (2, 1),
)


def reach_codes(way, origin):
    place = origin % 8
    codes = []
    for base in (0, 4):
        code = jnp.int32(0)
        for which in range(8):
            packed = sum(REACH[which][base + at][way] * 16**at for at in range(4))
            code = jnp.where(place == which, jnp.int32(packed), code)
        codes.append(code)
    return codes


def reach_of(codes, part):
    return codes[part // 4] // 16 ** (part % 4) % 16


def place_of(z):
    return z % 2 + 2 * (z // 4 % 2), z // 2 % 2


def z_of(dx, dy):
    return dx % 2 + 2 * dy + 4 * (dx // 2)


def lane_iota(rows=8):
    return lax.broadcasted_iota(jnp.int32, (rows, 128), 1)


def roll_lanes(value, shift):
    shift = shift % 128
    return pltpu.roll(value, shift, 1) if shift else value


def halves(value):
    high = value.astype(jnp.bfloat16)
    return high, (value - high.astype(jnp.float32)).astype(jnp.bfloat16)


def build_interp(me_dir, ids_ref, weights_ref, high_ref, low_ref):
    relative = (ids_ref[...] - 32 * me_dir + 2 + 512) % 512
    weights = weights_ref[...]
    row = lax.broadcasted_iota(jnp.int32, (128, 128), 0)
    for sub in range(4):
        wanted = (row - 32 * ((sub + me_dir) % 4) + 2 + 128) % 128
        total = jnp.zeros((128, 128), jnp.float32)
        for point in range(4):
            hit = relative[point : point + 1, :] == wanted
            total = total + jnp.where(hit, weights[point : point + 1, :], 0.0)
        inner = (wanted >= 2) & (wanted < 34)
        columns = slice(128 * sub, 128 * sub + 128)
        for at, value in (
            (0, jnp.where(inner, total, 0.0)),
            (128, jnp.where(inner, 0.0, total)),
        ):
            high, low = halves(value)
            high_ref[at : at + 128, columns] = high
            low_ref[at : at + 128, columns] = low


def pack_rows(shifted_ref, high_ref, low_ref, send_ref, chunk):
    high, low = halves(shifted_ref[...].reshape(128, 512))

    def times(left, right):
        return lax.dot_general(
            left, right, (((1,), (1,)), ((), ())), preferred_element_type=jnp.float32
        )

    product = times(high, high_ref[...]) + times(high, low_ref[...]) + times(low, high_ref[...])
    for owner in range(4):
        edges = None
        for line in range(4):
            at = 32 * owner + 8 * line
            send_ref[4 * chunk + owner, line] = product[at : at + 8, 0:128]
            piece = roll_lanes(product[at : at + 8, 128:256], 4 * line)
            edges = piece if edges is None else edges + piece
        send_ref[4 * chunk + owner, 4] = edges


def assemble(got_ref, out_ref):
    lane = lane_iota()
    group = lane // 32
    near = (lane + 2) % 32 < 4
    for sub in range(4):
        moved = (lane - 32 * sub + 128) % 128
        left_from = (moved + 2) // 32 % 4
        right_from = (moved + 96) // 32 % 4
        take_left = moved % 4 >= 2
        for quarter in range(4):
            left = right = None
            for source in range(4):
                left_at = 4 * quarter + source if source else 4 * ((quarter + 1) % 4)
                right_at = 4 * quarter + source if source < 3 else (4 * quarter + 15) % 16
                left_one, right_one = got_ref[left_at, 4], got_ref[right_at, 4]
                left = left_one if left is None else jnp.where(left_from == source, left_one, left)
                right = (
                    right_one if right is None else jnp.where(right_from == source, right_one, right)
                )
            edges = jnp.where(take_left, left, right)
            for line in range(4):
                main = None
                for at in range(4):
                    one = got_ref[4 * quarter + (at - sub) % 4, line]
                    main = one if main is None else jnp.where(group == at, one, main)
                main = roll_lanes(main, -32 * sub)
                extra = roll_lanes(edges, -(32 * sub + 4 * line))
                value = main + jnp.where(near, extra, 0.0)
                columns = slice(128 * quarter, 128 * quarter + 128)
                out_ref[4 * sub + line, 0, :, columns] = value[0:4]
                out_ref[4 * sub + line, 1, :, columns] = value[4:8]


def broadcast_table(raw_ref, table_ref, type_count):
    def step(tile, carry):
        rows = raw_ref[pl.ds(8 * tile, 8), :]
        for at in range(8):
            row = jnp.broadcast_to(rows[at : at + 1], (8, 128))
            table_ref[4 * tile + at // 2, at % 2] = row
        return carry

    lax.fori_loop(0, type_count // 4, step, 0)
    table_ref[type_count] = jnp.zeros((2, 8, 128), jnp.float32)


def stage_indices(
    own, type_count, ids_ref, types_ref, count_ref, child_ref, octant_ref, work_ref, stage_ref
):
    slots = ids_ref.shape[0]
    slot = lax.broadcasted_iota(jnp.int32, (slots, TILE), 0)
    box = lax.broadcasted_iota(jnp.int32, (slots, TILE), 1)
    live = slot < count_ref[...]
    work_ref[...] = jnp.zeros((128, 128), jnp.int32)
    source = jnp.where(live, ids_ref[...], own + box)
    work_ref[0:slots, 0:TILE] = source * 65536 + jnp.where(live, types_ref[...], type_count)
    stage_ref[0:TILE, :] = work_ref[...].T[0:TILE]
    upto = lax.broadcasted_iota(jnp.int32, (TILE, TILE), 0)
    which = lax.broadcasted_iota(jnp.int32, (TILE, TILE), 1)
    bounds = jnp.sum(jnp.where(which <= upto, child_ref[...], 0), axis=1, keepdims=True)
    for half in range(2):
        fine = lax.broadcasted_iota(jnp.int32, (TILE, 128), 1) + 128 * half
        parent = jnp.sum(jnp.where(bounds <= fine, 1, 0), axis=0, keepdims=True)
        parent = jnp.minimum(parent, TILE - 1)
        words = jnp.broadcast_to(parent * 16 + octant_ref[half : half + 1, :], (8, 128))
        at = TILE + 2 * half
        stage_ref[at : at + 1, :] = words[0:1]
        stage_ref[at + 1 : at + 2, :] = pltpu.roll(words, 64, 1)[0:1]


def build_phases(angle_ref, phase_ref):
    theta, phi = angle_ref[0:1, :], angle_ref[1:2, :]
    unit_x = jnp.sin(theta) * jnp.cos(phi)
    unit_y = jnp.sin(theta) * jnp.sin(phi)
    unit_z = jnp.cos(theta)
    octant = lax.broadcasted_iota(jnp.int32, (8, 128), 0)
    sign_x = 1.0 - 2.0 * (octant % 2).astype(jnp.float32)
    sign_y = 1.0 - 2.0 * (octant // 2 % 2).astype(jnp.float32)
    sign_z = 1.0 - 2.0 * (octant // 4).astype(jnp.float32)
    angle = wave_scale * (sign_x * unit_x + sign_y * unit_y + sign_z * unit_z)
    cosine, sine = jnp.cos(angle), jnp.sin(angle)
    for which in range(8):
        phase_ref[which, 0] = jnp.broadcast_to(cosine[which : which + 1], (8, 128))
        spread = jnp.broadcast_to(sine[which : which + 1], (8, 128))
        phase_ref[which, 1] = jnp.where(octant < 4, spread, -spread)


def translate_boxes(slots, index_ref, field_ref, table_ref, moved_ref):
    real_row = lax.broadcasted_iota(jnp.int32, (8, 128), 0) < 4

    def step(box, carry):
        sums = [None] * 4
        for slot in range(slots):
            packed = index_ref[box, slot]
            source = field_ref[packed >> 16]
            kind = packed & (table_ref.shape[0] - 1)
            for part in range(2):
                term = table_ref[kind, part] * source
                at = 2 * (slot % 2) + part
                sums[at] = term if sums[at] is None else sums[at] + term
        straight = sums[0] if sums[2] is None else sums[0] + sums[2]
        crossed = sums[1] if sums[3] is None else sums[1] + sums[3]
        crossed = pltpu.roll(crossed, 4, 0)
        value = straight + jnp.where(real_row, crossed, -crossed)
        moved_ref[box, 0] = value
        moved_ref[box, 1] = pltpu.roll(value, 4, 0)
        return carry

    lax.fori_loop(0, TILE, step, 0, unroll=2)


def shift_children(chunk, index_ref, moved_ref, phase_ref, shifted_ref):
    for owner in range(4):
        for fine in range(16):
            sub, line = fine // 4, fine % 4
            at = 16 * owner + fine
            packed = index_ref[TILE + chunk, at]
            parent, octant = (packed >> 4) & (TILE - 1), packed & 7
            value = (
                moved_ref[parent, 0] * phase_ref[octant, 0]
                + moved_ref[parent, 1] * phase_ref[octant, 1]
            )
            shifted_ref[4 * owner + line, :, 128 * sub : 128 * sub + 128] = value


def kernel(
    type_count,
    x_hbm,
    table_hbm,
    ids_hbm,
    types_hbm,
    count_hbm,
    child_hbm,
    octant_hbm,
    angles_hbm,
    stencil_hbm,
    weights_hbm,
    out_ref,
    field,
    raw,
    table,
    ids,
    types,
    count,
    child,
    octant,
    angles,
    stencil,
    weights,
    work,
    stage,
    index,
    phase,
    moved,
    shifted,
    matrix_high,
    matrix_low,
    outbox,
    inbox,
    load_sem,
    stage_sem,
    ring_send,
    ring_recv,
    side_send,
    side_recv,
    swap_send,
    swap_recv,
):
    me_box, me_dir = lax.axis_index("box"), lax.axis_index("dir")
    z, plane = me_box % RING, me_box // RING
    dx, dy = place_of(z)
    own = TILE * me_box
    slots = ids_hbm.shape[0]
    up, down = (z + 1) % RING, (z + RING - 1) % RING

    here = pl.ds(pl.multiple_of(128 * me_dir, 128), 128)
    loads = [
        pltpu.make_async_copy(src, dst, load_sem.at[at])
        for at, (src, dst) in enumerate(
            (
                (x_hbm, field.at[pl.ds(own, TILE)]),
                (table_hbm, raw),
                (ids_hbm, ids),
                (types_hbm, types),
                (count_hbm, count),
                (child_hbm, child),
                (octant_hbm, octant),
                (angles_hbm.at[:, here], angles),
                (stencil_hbm.at[:, here], stencil),
                (weights_hbm.at[:, here], weights),
            )
        )
    ]
    for load in loads:
        load.start()

    barrier = pltpu.get_barrier_semaphore()
    for place in (up, down):
        pl.semaphore_signal(
            barrier, inc=1, device_id={"box": RING * plane + place}, device_id_type=MESH
        )
    pl.semaphore_signal(
        barrier, inc=1, device_id={"box": RING * (1 - plane) + z}, device_id_type=MESH
    )
    for step in range(1, 16):
        pl.semaphore_signal(
            barrier, inc=1, device_id={"dir": (me_dir + step) % 16}, device_id_type=MESH
        )
    pl.semaphore_wait(barrier, 18)

    def rows_of(which_plane, origin, start, size):
        return field.at[pl.ds(TILE * (RING * which_plane + origin) + start, size)]

    def hop(way, step, part, origin, first=False):
        rows = rows_of(plane, origin, PART * part, PART)
        return pltpu.make_async_remote_copy(
            src_ref=x_hbm.at[pl.ds(PART * part, PART)] if first else rows,
            dst_ref=rows,
            send_sem=ring_send.at[way, part],
            recv_sem=ring_recv.at[way, step, part],
            device_id={"box": RING * plane + (down if way else up)},
            device_id_type=MESH,
        )

    def side(which_plane, origin, part, shift, size, slot, first=False):
        start = PART * part + shift
        rows = rows_of(which_plane, origin, start, size)
        return pltpu.make_async_remote_copy(
            src_ref=x_hbm.at[pl.ds(start, size)] if first else rows,
            dst_ref=rows,
            send_sem=side_send.at[slot],
            recv_sem=side_recv.at[slot],
            device_id={"box": RING * (1 - plane) + z},
            device_id_type=MESH,
        )

    first_codes = [reach_codes(way, z) for way in range(2)]
    for part, way in ORDER:

        @pl.when(reach_of(first_codes[way], part) > 0)
        def _():
            hop(way, 0, part, z, True).start()

    for part in range(PARTS):
        side(plane, z, part, 0, PART, part, True).start()

    for load in loads:
        load.wait()
    stage_indices(own, type_count, ids, types, count, child, octant, work, stage)
    to_index = pltpu.make_async_copy(stage, index, stage_sem)
    to_index.start()
    build_interp(me_dir, stencil, weights, matrix_high, matrix_low)
    build_phases(angles, phase)
    broadcast_table(raw, table, type_count)
    to_index.wait()

    def ring_step(step, carry):
        origins = [(z + RING - step) % RING, (z + step) % RING]
        codes = [reach_codes(way, origins[way]) for way in range(2)]
        spots = [place_of(origin) for origin in origins]
        for part, way in ORDER:
            origin, (from_x, from_y) = origins[way], spots[way]
            far = reach_of(codes[way], part)
            half_x, line = part // 2 % 2, part // 4 * 2 + part % 2
            near_y = same_y = from_y == dy
            base = jnp.where(origin // 8 == z // 8, 0, 20)
            if line == 0:
                near_y = near_y | (from_y > dy)
            if line == 3:
                near_y = near_y | (from_y < dy)

            @pl.when(step <= far)
            def _():
                hop(way, step - 1, part, origin).wait_recv()

                @pl.when(step < far)
                def _():
                    hop(way, step, part, origin).start()

                @pl.when(near_y & (from_x == dx))
                def _():
                    slot = base + jnp.where(same_y, part, 8 + half_x)
                    side(plane, origin, part, 0, PART, slot).start()

                @pl.when(near_y & (from_x - dx == 1 - 2 * half_x))
                def _():
                    slot = base + jnp.where(same_y, 10 + 4 * half_x + line, 18 + half_x)
                    side(plane, origin, part, 4 * half_x, 4, slot).start()

        return carry

    lax.fori_loop(1, HOPS + 1, ring_step, 0)

    def every_side(act, which_plane):
        for half in range(2):
            base = (z // 8 + half) % 2 * 8
            across = base + z_of(dx, 1 - dy)
            for part in range(PARTS):
                act(side(which_plane, base + z % 8, part, 0, PART, 20 * half + part))
            for half_x in range(2):
                slot = 20 * half + 8 + half_x
                act(side(which_plane, across, 5 * dy + 2 * half_x, 0, PART, slot))
            for half_x in range(2):
                to_x = dx + 1 - 2 * half_x

                @pl.when((to_x >= 0) & (to_x <= 3))
                def _():
                    shift = 4 * half_x
                    for line in range(4):
                        part = line // 2 * 4 + line % 2 + 2 * half_x
                        slot = 20 * half + 10 + 4 * half_x + line
                        act(side(which_plane, base + z_of(to_x, dy), part, shift, 4, slot))
                    part, slot = 5 * dy + 2 * half_x, 20 * half + 18 + half_x
                    act(side(which_plane, base + z_of(to_x, 1 - dy), part, shift, 4, slot))

    every_side(lambda copy: copy.wait_recv(), 1 - plane)

    translate_boxes(slots, index, field, table, moved)
    def swap(to, source):
        return pltpu.make_async_remote_copy(
            src_ref=outbox.at[to],
            dst_ref=inbox.at[source],
            send_sem=swap_send.at[to],
            recv_sem=swap_recv.at[source],
            device_id={"dir": to},
            device_id_type=MESH,
        )

    def pack(step, carry):
        chunk = (me_dir // 4 + 1 + step) % 4
        shift_children(chunk, index, moved, phase, shifted)
        pack_rows(shifted, matrix_high, matrix_low, outbox, chunk)
        for owner in range(4):
            to = 4 * chunk + owner

            @pl.when(to != me_dir)
            def _():
                swap(to, me_dir).start()

        return carry

    lax.fori_loop(0, 4, pack, 0)
    inbox[me_dir] = outbox[me_dir]

    every_side(lambda copy: copy.wait_send(), plane)

    for way in range(2):
        def count(step, sent):
            origin = (z + step) % RING if way else (z + RING - step) % RING
            codes = reach_codes(way, origin)
            return tuple(
                sent[part] + jnp.where(step < reach_of(codes, part), 1, 0) for part in range(PARTS)
            )

        sent = lax.fori_loop(0, HOPS, count, (jnp.int32(0),) * PARTS)
        for part in range(PARTS):
            for total in range(1, HOPS + 1):

                @pl.when(sent[part] == total)
                def _():
                    rows = field.at[pl.ds(0, PART * total)]
                    pltpu.make_async_remote_copy(
                        src_ref=rows,
                        dst_ref=rows,
                        send_sem=ring_send.at[way, part],
                        recv_sem=ring_recv.at[way, 0, part],
                        device_id={"box": RING * plane + (down if way else up)},
                        device_id_type=MESH,
                    ).wait_send()

    def receive(step, carry):
        other = (me_dir + step) % 16
        swap(other, other).wait_recv()
        swap(other, me_dir).wait_send()
        return carry

    lax.fori_loop(1, 16, receive, 0)
    assemble(inbox, out_ref)


def per_device(
    coarse_field,
    trans_table,
    partner_ids,
    partner_types,
    partner_count,
    child_count,
    child_octant,
    dir_angles,
    stencil_ids,
    stencil_weights,
):
    type_count = trans_table.shape[0]
    slots = partner_ids.shape[1]
    f32, i32 = jnp.float32, jnp.int32
    vmem, dma = pltpu.VMEM, pltpu.SemaphoreType.DMA
    return pl.pallas_call(
        functools.partial(kernel, type_count),
        out_shape=jax.ShapeDtypeStruct((16, 2, 4, 512), f32),
        in_specs=[pl.BlockSpec(memory_space=pl.ANY)] * 10,
        out_specs=pl.BlockSpec(memory_space=pltpu.VMEM),
        scratch_shapes=[
            vmem((2048, 8, 128), f32),
            vmem((2 * type_count, 128), f32),
            vmem((512, 2, 8, 128), f32),
            vmem((slots, TILE), i32),
            vmem((slots, TILE), i32),
            vmem((1, TILE), i32),
            vmem((1, TILE), i32),
            vmem((2, 128), i32),
            vmem((2, 128), f32),
            vmem((4, 128), i32),
            vmem((4, 128), f32),
            vmem((128, 128), i32),
            vmem((72, 128), i32),
            pltpu.SMEM((72, 128), i32),
            vmem((8, 2, 8, 128), f32),
            vmem((TILE, 2, 8, 128), f32),
            vmem((16, 8, 512), f32),
            vmem((256, 512), jnp.bfloat16),
            vmem((256, 512), jnp.bfloat16),
            vmem((16, 5, 8, 128), f32),
            vmem((16, 5, 8, 128), f32),
            dma((10,)),
            dma,
            dma((2, PARTS)),
            dma((2, HOPS, PARTS)),
            dma((40,)),
            dma((40,)),
            dma((16,)),
            dma((16,)),
        ],
        compiler_params=pltpu.CompilerParams(collective_id=0, has_side_effects=True),
    )(
        coarse_field.reshape(TILE, 8, 128),
        trans_table.reshape(2 * type_count, 128),
        partner_ids.T,
        partner_types.T,
        partner_count.reshape(1, TILE),
        child_count.reshape(1, TILE),
        child_octant.reshape(2, 128),
        dir_angles,
        stencil_ids.T,
        stencil_weights.T,
    )


def solution(mesh):
    placed = (
        P("box", None, None, "dir"),
        P(None, None, "dir"),
        P("box", None),
        P("box", None),
        P("box"),
        P("box"),
        P("box"),
        P(),
        P(),
        P(),
    )
    return jax.shard_map(
        per_device,
        mesh=mesh,
        in_specs=placed,
        out_specs=P(("box", "dir"), None, None, None),
        check_vma=False,
    )
```

```python
import functools

import jax
import jax.numpy as jnp
from jax import lax
from jax.experimental import pallas as pl
from jax.experimental.pallas import tpu as pltpu
from jax.sharding import PartitionSpec as P

MESH = pl.DeviceIdType.MESH
wave_scale = 3.0

RING = 16
HOPS = 8
TILE = 64
PART = 8
PARTS = 8

REACH = (
    ((8, 0), (8, 0), (1, 8), (1, 8), (8, 0), (2, 8), (1, 8), (3, 8)),
    ((8, 1), (8, 1), (3, 8), (3, 8), (8, 1), (8, 7), (3, 8), (8, 6)),
    ((8, 2), (8, 0), (8, 7), (1, 8), (8, 0), (0, 8), (1, 8), (1, 8)),
    ((8, 3), (8, 1), (6, 8), (3, 8), (8, 1), (8, 1), (8, 5), (3, 8)),
    ((8, 3), (8, 3), (1, 8), (1, 8), (8, 3), (8, 6), (1, 8), (3, 8)),
    ((8, 1), (8, 1), (0, 8), (0, 8), (8, 1), (8, 7), (0, 8), (2, 8)),
    ((6, 8), (8, 3), (8, 7), (1, 8), (8, 3), (8, 3), (1, 8), (1, 8)),
    ((8, 3), (8, 1), (8, 2), (0, 8), (8, 1), (8, 1), (0, 8), (0, 8)),
)

ORDER = (
    (5, 0),
    (3, 1),
    (4, 0),
    (0, 1),
    (0, 0),
    (7, 1),
    (7, 0),
    (6, 0),
    (1, 1),
    (4, 1),
    (2, 0),
    (6, 1),
    (3, 0),
    (1, 0),
    (5, 1),
    (2, 1),
)


def reach_codes(way, origin):
    place = origin % 8
    codes = []
    for base in (0, 4):
        code = jnp.int32(0)
        for which in range(8):
            packed = sum(REACH[which][base + at][way] * 16**at for at in range(4))
            code = jnp.where(place == which, jnp.int32(packed), code)
        codes.append(code)
    return codes


def reach_of(codes, part):
    return codes[part // 4] // 16 ** (part % 4) % 16


def place_of(z):
    return z % 2 + 2 * (z // 4 % 2), z // 2 % 2


def z_of(dx, dy):
    return dx % 2 + 2 * dy + 4 * (dx // 2)


def lane_iota(rows=8):
    return lax.broadcasted_iota(jnp.int32, (rows, 128), 1)


def roll_lanes(value, shift):
    shift = shift % 128
    return pltpu.roll(value, shift, 1) if shift else value


def halves(value):
    high = value.astype(jnp.bfloat16)
    return high, (value - high.astype(jnp.float32)).astype(jnp.bfloat16)


def build_interp(me_dir, ids_ref, weights_ref, high_ref, low_ref):
    relative = (ids_ref[...] - 32 * me_dir + 2 + 512) % 512
    weights = weights_ref[...]
    row = lax.broadcasted_iota(jnp.int32, (128, 128), 0)
    for sub in range(4):
        wanted = (row - 32 * ((sub + me_dir) % 4) + 2 + 128) % 128
        total = jnp.zeros((128, 128), jnp.float32)
        for point in range(4):
            hit = relative[point : point + 1, :] == wanted
            total = total + jnp.where(hit, weights[point : point + 1, :], 0.0)
        inner = (wanted >= 2) & (wanted < 34)
        columns = slice(128 * sub, 128 * sub + 128)
        for at, value in (
            (0, jnp.where(inner, total, 0.0)),
            (128, jnp.where(inner, 0.0, total)),
        ):
            high, low = halves(value)
            high_ref[at : at + 128, columns] = high
            low_ref[at : at + 128, columns] = low


def pack_rows(shifted_ref, high_ref, low_ref, send_ref, chunk):
    high, low = halves(shifted_ref[...].reshape(128, 512))

    def times(left, right):
        return lax.dot_general(
            left, right, (((1,), (1,)), ((), ())), preferred_element_type=jnp.float32
        )

    product = times(high, high_ref[...]) + times(high, low_ref[...]) + times(low, high_ref[...])
    for owner in range(4):
        edges = None
        for line in range(4):
            at = 32 * owner + 8 * line
            send_ref[4 * chunk + owner, line] = product[at : at + 8, 0:128]
            piece = roll_lanes(product[at : at + 8, 128:256], 4 * line)
            edges = piece if edges is None else edges + piece
        send_ref[4 * chunk + owner, 4] = edges


def assemble(got_ref, out_ref):
    lane = lane_iota()
    group = lane // 32
    near = (lane + 2) % 32 < 4
    for sub in range(4):
        moved = (lane - 32 * sub + 128) % 128
        left_from = (moved + 2) // 32 % 4
        right_from = (moved + 96) // 32 % 4
        take_left = moved % 4 >= 2
        for quarter in range(4):
            left = right = None
            for source in range(4):
                left_at = 4 * quarter + source if source else 4 * ((quarter + 1) % 4)
                right_at = 4 * quarter + source if source < 3 else (4 * quarter + 15) % 16
                left_one, right_one = got_ref[left_at, 4], got_ref[right_at, 4]
                left = left_one if left is None else jnp.where(left_from == source, left_one, left)
                right = (
                    right_one if right is None else jnp.where(right_from == source, right_one, right)
                )
            edges = jnp.where(take_left, left, right)
            for line in range(4):
                main = None
                for at in range(4):
                    one = got_ref[4 * quarter + (at - sub) % 4, line]
                    main = one if main is None else jnp.where(group == at, one, main)
                main = roll_lanes(main, -32 * sub)
                extra = roll_lanes(edges, -(32 * sub + 4 * line))
                value = main + jnp.where(near, extra, 0.0)
                columns = slice(128 * quarter, 128 * quarter + 128)
                out_ref[4 * sub + line, 0, :, columns] = value[0:4]
                out_ref[4 * sub + line, 1, :, columns] = value[4:8]


def fetch_operators(slots, box, index_ref, raw_ref, rows_ref):
    for slot in range(slots):
        rows_ref[box, 2 * slot : 2 * slot + 2, :] = raw_ref[index_ref[box, 32 + slot]]


def stage_indices(
    own, type_count, ids_ref, types_ref, count_ref, child_ref, octant_ref, work_ref, stage_ref
):
    slots = ids_ref.shape[0]
    slot = lax.broadcasted_iota(jnp.int32, (slots, TILE), 0)
    box = lax.broadcasted_iota(jnp.int32, (slots, TILE), 1)
    live = slot < count_ref[...]
    work_ref[...] = jnp.zeros((128, 128), jnp.int32)
    source = jnp.where(live, ids_ref[...], own + box)
    work_ref[0:slots, 0:TILE] = source
    work_ref[32 : 32 + slots, 0:TILE] = jnp.where(live, types_ref[...], type_count)
    stage_ref[0:TILE, :] = work_ref[...].T[0:TILE]
    upto = lax.broadcasted_iota(jnp.int32, (TILE, TILE), 0)
    which = lax.broadcasted_iota(jnp.int32, (TILE, TILE), 1)
    bounds = jnp.sum(jnp.where(which <= upto, child_ref[...], 0), axis=1, keepdims=True)
    for half in range(2):
        fine = lax.broadcasted_iota(jnp.int32, (TILE, 128), 1) + 128 * half
        parent = jnp.sum(jnp.where(bounds <= fine, 1, 0), axis=0, keepdims=True)
        parent = jnp.minimum(parent, TILE - 1)
        words = jnp.broadcast_to(parent * 16 + octant_ref[half : half + 1, :], (8, 128))
        at = TILE + 2 * half
        stage_ref[at : at + 1, :] = words[0:1]
        stage_ref[at + 1 : at + 2, :] = pltpu.roll(words, 64, 1)[0:1]


def build_phases(angle_ref, phase_ref):
    theta, phi = angle_ref[0:1, :], angle_ref[1:2, :]
    unit_x = jnp.sin(theta) * jnp.cos(phi)
    unit_y = jnp.sin(theta) * jnp.sin(phi)
    unit_z = jnp.cos(theta)
    octant = lax.broadcasted_iota(jnp.int32, (8, 128), 0)
    sign_x = 1.0 - 2.0 * (octant % 2).astype(jnp.float32)
    sign_y = 1.0 - 2.0 * (octant // 2 % 2).astype(jnp.float32)
    sign_z = 1.0 - 2.0 * (octant // 4).astype(jnp.float32)
    angle = wave_scale * (sign_x * unit_x + sign_y * unit_y + sign_z * unit_z)
    cosine, sine = jnp.cos(angle), jnp.sin(angle)
    for which in range(8):
        phase_ref[which, 0] = jnp.broadcast_to(cosine[which : which + 1], (8, 128))
        spread = jnp.broadcast_to(sine[which : which + 1], (8, 128))
        phase_ref[which, 1] = jnp.where(octant < 4, spread, -spread)


def translate_boxes(slots, index_ref, field_ref, rows_ref, moved_ref):
    real_row = lax.broadcasted_iota(jnp.int32, (8, 128), 0) < 4

    def step(box, carry):
        sums = [None] * 4
        for slot in range(slots):
            source = field_ref[index_ref[box, slot]]
            for part in range(2):
                row = rows_ref[box, 2 * slot + part : 2 * slot + part + 1, :]
                term = jnp.broadcast_to(row, (8, 128)) * source
                at = 2 * (slot % 2) + part
                sums[at] = term if sums[at] is None else sums[at] + term
        straight = sums[0] if sums[2] is None else sums[0] + sums[2]
        crossed = sums[1] if sums[3] is None else sums[1] + sums[3]
        crossed = pltpu.roll(crossed, 4, 0)
        value = straight + jnp.where(real_row, crossed, -crossed)
        moved_ref[box, 0] = value
        moved_ref[box, 1] = pltpu.roll(value, 4, 0)
        return carry

    lax.fori_loop(0, TILE, step, 0, unroll=2)


def shift_children(chunk, index_ref, moved_ref, phase_ref, shifted_ref):
    for owner in range(4):
        for fine in range(16):
            sub, line = fine // 4, fine % 4
            at = 16 * owner + fine
            packed = index_ref[TILE + chunk, at]
            parent, octant = (packed >> 4) & (TILE - 1), packed & 7
            value = (
                moved_ref[parent, 0] * phase_ref[octant, 0]
                + moved_ref[parent, 1] * phase_ref[octant, 1]
            )
            shifted_ref[4 * owner + line, :, 128 * sub : 128 * sub + 128] = value


def kernel(
    type_count,
    x_hbm,
    table_hbm,
    ids_hbm,
    types_hbm,
    count_hbm,
    child_hbm,
    octant_hbm,
    angles_hbm,
    stencil_hbm,
    weights_hbm,
    out_ref,
    field,
    raw,
    rows,
    ids,
    types,
    count,
    child,
    octant,
    angles,
    stencil,
    weights,
    work,
    stage,
    index,
    phase,
    moved,
    shifted,
    matrix_high,
    matrix_low,
    outbox,
    inbox,
    load_sem,
    stage_sem,
    ring_send,
    ring_recv,
    side_send,
    side_recv,
    swap_send,
    swap_recv,
):
    me_box, me_dir = lax.axis_index("box"), lax.axis_index("dir")
    z, plane = me_box % RING, me_box // RING
    dx, dy = place_of(z)
    own = TILE * me_box
    slots = ids_hbm.shape[0]
    up, down = (z + 1) % RING, (z + RING - 1) % RING

    here = pl.ds(pl.multiple_of(128 * me_dir, 128), 128)
    loads = [
        pltpu.make_async_copy(src, dst, load_sem.at[at])
        for at, (src, dst) in enumerate(
            (
                (x_hbm, field.at[pl.ds(own, TILE)]),
                (table_hbm, raw.at[pl.ds(0, type_count)]),
                (ids_hbm, ids),
                (types_hbm, types),
                (count_hbm, count),
                (child_hbm, child),
                (octant_hbm, octant),
                (angles_hbm.at[:, here], angles),
                (stencil_hbm.at[:, here], stencil),
                (weights_hbm.at[:, here], weights),
            )
        )
    ]
    for load in loads:
        load.start()

    barrier = pltpu.get_barrier_semaphore()
    for place in (up, down):
        pl.semaphore_signal(
            barrier, inc=1, device_id={"box": RING * plane + place}, device_id_type=MESH
        )
    pl.semaphore_signal(
        barrier, inc=1, device_id={"box": RING * (1 - plane) + z}, device_id_type=MESH
    )
    for step in range(1, 16):
        pl.semaphore_signal(
            barrier, inc=1, device_id={"dir": (me_dir + step) % 16}, device_id_type=MESH
        )
    pl.semaphore_wait(barrier, 18)

    def rows_of(which_plane, origin, start, size):
        return field.at[pl.ds(TILE * (RING * which_plane + origin) + start, size)]

    def hop(way, step, part, origin, first=False):
        here = rows_of(plane, origin, PART * part, PART)
        return pltpu.make_async_remote_copy(
            src_ref=x_hbm.at[pl.ds(PART * part, PART)] if first else here,
            dst_ref=here,
            send_sem=ring_send.at[way, part],
            recv_sem=ring_recv.at[way, step, part],
            device_id={"box": RING * plane + (down if way else up)},
            device_id_type=MESH,
        )

    def side(which_plane, origin, part, shift, size, slot, first=False):
        start = PART * part + shift
        rows = rows_of(which_plane, origin, start, size)
        return pltpu.make_async_remote_copy(
            src_ref=x_hbm.at[pl.ds(start, size)] if first else rows,
            dst_ref=rows,
            send_sem=side_send.at[slot],
            recv_sem=side_recv.at[slot],
            device_id={"box": RING * (1 - plane) + z},
            device_id_type=MESH,
        )

    first_codes = [reach_codes(way, z) for way in range(2)]
    for part, way in ORDER:

        @pl.when(reach_of(first_codes[way], part) > 0)
        def _():
            hop(way, 0, part, z, True).start()

    for part in range(PARTS):
        side(plane, z, part, 0, PART, part, True).start()

    for load in loads:
        load.wait()
    stage_indices(own, type_count, ids, types, count, child, octant, work, stage)
    to_index = pltpu.make_async_copy(stage, index, stage_sem)
    to_index.start()
    build_interp(me_dir, stencil, weights, matrix_high, matrix_low)
    build_phases(angles, phase)
    raw[type_count] = jnp.zeros((2, 128), jnp.float32)
    to_index.wait()

    def ring_step(step, carry):
        origins = [(z + RING - step) % RING, (z + step) % RING]
        codes = [reach_codes(way, origins[way]) for way in range(2)]
        spots = [place_of(origin) for origin in origins]
        for turn, (part, way) in enumerate(ORDER):
            origin, (from_x, from_y) = origins[way], spots[way]
            far = reach_of(codes[way], part)
            half_x, line = part // 2 % 2, part // 4 * 2 + part % 2
            near_y = same_y = from_y == dy
            base = jnp.where(origin // 8 == z // 8, 0, 20)
            if line == 0:
                near_y = near_y | (from_y > dy)
            if line == 3:
                near_y = near_y | (from_y < dy)

            @pl.when(step <= far)
            def _():
                hop(way, step - 1, part, origin).wait_recv()

                @pl.when(step < far)
                def _():
                    hop(way, step, part, origin).start()

                @pl.when(near_y & (from_x == dx))
                def _():
                    slot = base + jnp.where(same_y, part, 8 + half_x)
                    side(plane, origin, part, 0, PART, slot).start()

                @pl.when(near_y & (from_x - dx == 1 - 2 * half_x))
                def _():
                    slot = base + jnp.where(same_y, 10 + 4 * half_x + line, 18 + half_x)
                    side(plane, origin, part, 4 * half_x, 4, slot).start()

            if turn % 2:
                fetch_operators(slots, 8 * (step - 1) + turn // 2, index, raw, rows)

        return carry

    lax.fori_loop(1, HOPS + 1, ring_step, 0)

    def every_side(act, which_plane):
        for half in range(2):
            base = (z // 8 + half) % 2 * 8
            across = base + z_of(dx, 1 - dy)
            for part in range(PARTS):
                act(side(which_plane, base + z % 8, part, 0, PART, 20 * half + part))
            for half_x in range(2):
                slot = 20 * half + 8 + half_x
                act(side(which_plane, across, 5 * dy + 2 * half_x, 0, PART, slot))
            for half_x in range(2):
                to_x = dx + 1 - 2 * half_x

                @pl.when((to_x >= 0) & (to_x <= 3))
                def _():
                    shift = 4 * half_x
                    for line in range(4):
                        part = line // 2 * 4 + line % 2 + 2 * half_x
                        slot = 20 * half + 10 + 4 * half_x + line
                        act(side(which_plane, base + z_of(to_x, dy), part, shift, 4, slot))
                    part, slot = 5 * dy + 2 * half_x, 20 * half + 18 + half_x
                    act(side(which_plane, base + z_of(to_x, 1 - dy), part, shift, 4, slot))

    every_side(lambda copy: copy.wait_recv(), 1 - plane)

    translate_boxes(slots, index, field, rows, moved)
    def swap(to, source):
        return pltpu.make_async_remote_copy(
            src_ref=outbox.at[to],
            dst_ref=inbox.at[source],
            send_sem=swap_send.at[to],
            recv_sem=swap_recv.at[source],
            device_id={"dir": to},
            device_id_type=MESH,
        )

    def pack(step, carry):
        chunk = (me_dir // 4 + 1 + step) % 4
        shift_children(chunk, index, moved, phase, shifted)
        pack_rows(shifted, matrix_high, matrix_low, outbox, chunk)
        for owner in range(4):
            to = 4 * chunk + owner

            @pl.when(to != me_dir)
            def _():
                swap(to, me_dir).start()

        return carry

    lax.fori_loop(0, 4, pack, 0)
    inbox[me_dir] = outbox[me_dir]

    every_side(lambda copy: copy.wait_send(), plane)

    for way in range(2):
        def count(step, sent):
            origin = (z + step) % RING if way else (z + RING - step) % RING
            codes = reach_codes(way, origin)
            return tuple(
                sent[part] + jnp.where(step < reach_of(codes, part), 1, 0) for part in range(PARTS)
            )

        sent = lax.fori_loop(0, HOPS, count, (jnp.int32(0),) * PARTS)
        for part in range(PARTS):
            for total in range(1, HOPS + 1):

                @pl.when(sent[part] == total)
                def _():
                    rows = field.at[pl.ds(0, PART * total)]
                    pltpu.make_async_remote_copy(
                        src_ref=rows,
                        dst_ref=rows,
                        send_sem=ring_send.at[way, part],
                        recv_sem=ring_recv.at[way, 0, part],
                        device_id={"box": RING * plane + (down if way else up)},
                        device_id_type=MESH,
                    ).wait_send()

    def receive(step, carry):
        other = (me_dir + step) % 16
        swap(other, other).wait_recv()
        swap(other, me_dir).wait_send()
        return carry

    lax.fori_loop(1, 16, receive, 0)
    assemble(inbox, out_ref)


def per_device(
    coarse_field,
    trans_table,
    partner_ids,
    partner_types,
    partner_count,
    child_count,
    child_octant,
    dir_angles,
    stencil_ids,
    stencil_weights,
):
    type_count = trans_table.shape[0]
    slots = partner_ids.shape[1]
    f32, i32 = jnp.float32, jnp.int32
    vmem, dma = pltpu.VMEM, pltpu.SemaphoreType.DMA
    return pl.pallas_call(
        functools.partial(kernel, type_count),
        out_shape=jax.ShapeDtypeStruct((16, 2, 4, 512), f32),
        in_specs=[pl.BlockSpec(memory_space=pl.ANY)] * 10,
        out_specs=pl.BlockSpec(memory_space=pltpu.VMEM),
        scratch_shapes=[
            vmem((2048, 8, 128), f32),
            vmem((type_count + 4, 2, 128), f32),
            vmem((TILE, 64, 128), f32),
            vmem((slots, TILE), i32),
            vmem((slots, TILE), i32),
            vmem((1, TILE), i32),
            vmem((1, TILE), i32),
            vmem((2, 128), i32),
            vmem((2, 128), f32),
            vmem((4, 128), i32),
            vmem((4, 128), f32),
            vmem((128, 128), i32),
            vmem((72, 128), i32),
            pltpu.SMEM((72, 128), i32),
            vmem((8, 2, 8, 128), f32),
            vmem((TILE, 2, 8, 128), f32),
            vmem((16, 8, 512), f32),
            vmem((256, 512), jnp.bfloat16),
            vmem((256, 512), jnp.bfloat16),
            vmem((16, 5, 8, 128), f32),
            vmem((16, 5, 8, 128), f32),
            dma((10,)),
            dma,
            dma((2, PARTS)),
            dma((2, HOPS, PARTS)),
            dma((40,)),
            dma((40,)),
            dma((16,)),
            dma((16,)),
        ],
        compiler_params=pltpu.CompilerParams(collective_id=0, has_side_effects=True),
    )(
        coarse_field.reshape(TILE, 8, 128),
        trans_table,
        partner_ids.T,
        partner_types.T,
        partner_count.reshape(1, TILE),
        child_count.reshape(1, TILE),
        child_octant.reshape(2, 128),
        dir_angles,
        stencil_ids.T,
        stencil_weights.T,
    )


def solution(mesh):
    placed = (
        P("box", None, None, "dir"),
        P(None, None, "dir"),
        P("box", None),
        P("box", None),
        P("box"),
        P("box"),
        P("box"),
        P(),
        P(),
        P(),
    )
    return jax.shard_map(
        per_device,
        mesh=mesh,
        in_specs=placed,
        out_specs=P(("box", "dir"), None, None, None),
        check_vma=False,
    )
```

```python
import functools

import jax
import jax.numpy as jnp
from jax import lax
from jax.experimental import pallas as pl
from jax.experimental.pallas import tpu as pltpu
from jax.sharding import PartitionSpec as P

MESH = pl.DeviceIdType.MESH
wave_scale = 3.0

RING = 16
HOPS = 8
TILE = 64
PART = 8
PARTS = 8

REACH = (
    ((8, 0), (8, 0), (1, 8), (1, 8), (8, 0), (2, 8), (1, 8), (3, 8)),
    ((8, 1), (8, 1), (3, 8), (3, 8), (8, 1), (7, 8), (3, 8), (8, 6)),
    ((8, 2), (8, 0), (7, 8), (1, 8), (8, 0), (8, 0), (1, 8), (1, 8)),
    ((8, 3), (8, 1), (6, 8), (3, 8), (8, 1), (8, 1), (3, 8), (3, 8)),
    ((8, 3), (8, 3), (1, 8), (1, 8), (5, 8), (8, 6), (1, 8), (3, 8)),
    ((8, 1), (8, 1), (8, 0), (0, 8), (8, 1), (7, 8), (0, 8), (2, 8)),
    ((6, 8), (8, 3), (8, 7), (1, 8), (8, 3), (8, 3), (1, 8), (1, 8)),
    ((8, 3), (8, 1), (8, 2), (0, 8), (8, 1), (8, 1), (0, 8), (0, 8)),
)

ORDER = (
    (2, 1),
    (4, 1),
    (2, 0),
    (7, 0),
    (6, 1),
    (1, 0),
    (5, 1),
    (3, 0),
    (4, 0),
    (3, 1),
    (1, 1),
    (0, 1),
    (0, 0),
    (7, 1),
    (5, 0),
    (6, 0),
)


def reach_codes(way, origin):
    place = origin % 8
    codes = []
    for base in (0, 4):
        code = jnp.int32(0)
        for which in range(8):
            packed = sum(REACH[which][base + at][way] * 16**at for at in range(4))
            code = jnp.where(place == which, jnp.int32(packed), code)
        codes.append(code)
    return codes


def reach_of(codes, part):
    return codes[part // 4] // 16 ** (part % 4) % 16


def place_of(z):
    return z % 2 + 2 * (z // 4 % 2), z // 2 % 2


def z_of(dx, dy):
    return dx % 2 + 2 * dy + 4 * (dx // 2)


def lane_iota(rows=8):
    return lax.broadcasted_iota(jnp.int32, (rows, 128), 1)


def roll_lanes(value, shift):
    shift = shift % 128
    return pltpu.roll(value, shift, 1) if shift else value


def halves(value):
    high = value.astype(jnp.bfloat16)
    return high, (value - high.astype(jnp.float32)).astype(jnp.bfloat16)


def build_interp(me_dir, ids_ref, weights_ref, high_ref, low_ref):
    relative = (ids_ref[...] - 32 * me_dir + 2 + 512) % 512
    weights = weights_ref[...]
    row = lax.broadcasted_iota(jnp.int32, (128, 128), 0)
    for sub in range(4):
        wanted = (row - 32 * ((sub + me_dir) % 4) + 2 + 128) % 128
        total = jnp.zeros((128, 128), jnp.float32)
        for point in range(4):
            hit = relative[point : point + 1, :] == wanted
            total = total + jnp.where(hit, weights[point : point + 1, :], 0.0)
        inner = (wanted >= 2) & (wanted < 34)
        columns = slice(128 * sub, 128 * sub + 128)
        for at, value in (
            (0, jnp.where(inner, total, 0.0)),
            (128, jnp.where(inner, 0.0, total)),
        ):
            high, low = halves(value)
            high_ref[at : at + 128, columns] = high
            low_ref[at : at + 128, columns] = low


def pack_rows(shifted_ref, high_ref, low_ref, send_ref, chunk):
    high, low = halves(shifted_ref[...].reshape(128, 512))

    def times(left, right):
        return lax.dot_general(
            left, right, (((1,), (1,)), ((), ())), preferred_element_type=jnp.float32
        )

    product = times(high, high_ref[...]) + times(high, low_ref[...]) + times(low, high_ref[...])
    for owner in range(4):
        edges = None
        for line in range(4):
            at = 32 * owner + 8 * line
            send_ref[4 * chunk + owner, line] = product[at : at + 8, 0:128]
            piece = roll_lanes(product[at : at + 8, 128:256], 4 * line)
            edges = piece if edges is None else edges + piece
        send_ref[4 * chunk + owner, 4] = edges


def assemble(got_ref, out_ref):
    lane = lane_iota()
    group = lane // 32
    near = (lane + 2) % 32 < 4
    for sub in range(4):
        moved = (lane - 32 * sub + 128) % 128
        left_from = (moved + 2) // 32 % 4
        right_from = (moved + 96) // 32 % 4
        take_left = moved % 4 >= 2
        for quarter in range(4):
            left = right = None
            for source in range(4):
                left_at = 4 * quarter + source if source else 4 * ((quarter + 1) % 4)
                right_at = 4 * quarter + source if source < 3 else (4 * quarter + 15) % 16
                left_one, right_one = got_ref[left_at, 4], got_ref[right_at, 4]
                left = left_one if left is None else jnp.where(left_from == source, left_one, left)
                right = (
                    right_one if right is None else jnp.where(right_from == source, right_one, right)
                )
            edges = jnp.where(take_left, left, right)
            for line in range(4):
                main = None
                for at in range(4):
                    one = got_ref[4 * quarter + (at - sub) % 4, line]
                    main = one if main is None else jnp.where(group == at, one, main)
                main = roll_lanes(main, -32 * sub)
                extra = roll_lanes(edges, -(32 * sub + 4 * line))
                value = main + jnp.where(near, extra, 0.0)
                columns = slice(128 * quarter, 128 * quarter + 128)
                out_ref[4 * sub + line, 0, :, columns] = value[0:4]
                out_ref[4 * sub + line, 1, :, columns] = value[4:8]


def fetch_operators(slots, box, index_ref, raw_ref, rows_ref):
    for slot in range(slots):
        rows_ref[box, 2 * slot : 2 * slot + 2, :] = raw_ref[index_ref[box, 32 + slot]]


def stage_indices(
    own, type_count, ids_ref, types_ref, count_ref, child_ref, octant_ref, work_ref, stage_ref
):
    slots = ids_ref.shape[0]
    slot = lax.broadcasted_iota(jnp.int32, (slots, TILE), 0)
    box = lax.broadcasted_iota(jnp.int32, (slots, TILE), 1)
    live = slot < count_ref[...]
    work_ref[...] = jnp.zeros((128, 128), jnp.int32)
    source = jnp.where(live, ids_ref[...], own + box)
    work_ref[0:slots, 0:TILE] = source
    work_ref[32 : 32 + slots, 0:TILE] = jnp.where(live, types_ref[...], type_count)
    stage_ref[0:TILE, :] = work_ref[...].T[0:TILE]
    upto = lax.broadcasted_iota(jnp.int32, (TILE, TILE), 0)
    which = lax.broadcasted_iota(jnp.int32, (TILE, TILE), 1)
    bounds = jnp.sum(jnp.where(which <= upto, child_ref[...], 0), axis=1, keepdims=True)
    for half in range(2):
        fine = lax.broadcasted_iota(jnp.int32, (TILE, 128), 1) + 128 * half
        parent = jnp.sum(jnp.where(bounds <= fine, 1, 0), axis=0, keepdims=True)
        parent = jnp.minimum(parent, TILE - 1)
        words = jnp.broadcast_to(parent * 16 + octant_ref[half : half + 1, :], (8, 128))
        at = TILE + 2 * half
        stage_ref[at : at + 1, :] = words[0:1]
        stage_ref[at + 1 : at + 2, :] = pltpu.roll(words, 64, 1)[0:1]


def build_phases(angle_ref, phase_ref):
    theta, phi = angle_ref[0:1, :], angle_ref[1:2, :]
    unit_x = jnp.sin(theta) * jnp.cos(phi)
    unit_y = jnp.sin(theta) * jnp.sin(phi)
    unit_z = jnp.cos(theta)
    octant = lax.broadcasted_iota(jnp.int32, (8, 128), 0)
    sign_x = 1.0 - 2.0 * (octant % 2).astype(jnp.float32)
    sign_y = 1.0 - 2.0 * (octant // 2 % 2).astype(jnp.float32)
    sign_z = 1.0 - 2.0 * (octant // 4).astype(jnp.float32)
    angle = wave_scale * (sign_x * unit_x + sign_y * unit_y + sign_z * unit_z)
    cosine, sine = jnp.cos(angle), jnp.sin(angle)
    for which in range(8):
        phase_ref[which, 0] = jnp.broadcast_to(cosine[which : which + 1], (8, 128))
        spread = jnp.broadcast_to(sine[which : which + 1], (8, 128))
        phase_ref[which, 1] = jnp.where(octant < 4, spread, -spread)


def translate_boxes(slots, index_ref, field_ref, rows_ref, moved_ref):
    real_row = lax.broadcasted_iota(jnp.int32, (8, 128), 0) < 4

    def step(box, carry):
        sums = [None] * 4
        for slot in range(slots):
            source = field_ref[index_ref[box, slot]]
            for part in range(2):
                row = rows_ref[box, 2 * slot + part : 2 * slot + part + 1, :]
                term = jnp.broadcast_to(row, (8, 128)) * source
                at = 2 * (slot % 2) + part
                sums[at] = term if sums[at] is None else sums[at] + term
        straight = sums[0] if sums[2] is None else sums[0] + sums[2]
        crossed = sums[1] if sums[3] is None else sums[1] + sums[3]
        crossed = pltpu.roll(crossed, 4, 0)
        value = straight + jnp.where(real_row, crossed, -crossed)
        moved_ref[box, 0] = value
        moved_ref[box, 1] = pltpu.roll(value, 4, 0)
        return carry

    lax.fori_loop(0, TILE, step, 0, unroll=2)


def shift_children(chunk, index_ref, moved_ref, phase_ref, shifted_ref):
    for owner in range(4):
        for fine in range(16):
            sub, line = fine // 4, fine % 4
            at = 16 * owner + fine
            packed = index_ref[TILE + chunk, at]
            parent, octant = (packed >> 4) & (TILE - 1), packed & 7
            value = (
                moved_ref[parent, 0] * phase_ref[octant, 0]
                + moved_ref[parent, 1] * phase_ref[octant, 1]
            )
            shifted_ref[4 * owner + line, :, 128 * sub : 128 * sub + 128] = value


def kernel(
    type_count,
    x_hbm,
    table_hbm,
    ids_hbm,
    types_hbm,
    count_hbm,
    child_hbm,
    octant_hbm,
    angles_hbm,
    stencil_hbm,
    weights_hbm,
    out_ref,
    field,
    raw,
    rows,
    ids,
    types,
    count,
    child,
    octant,
    angles,
    stencil,
    weights,
    work,
    stage,
    index,
    phase,
    moved,
    shifted,
    matrix_high,
    matrix_low,
    outbox,
    inbox,
    load_sem,
    stage_sem,
    ring_send,
    ring_recv,
    side_send,
    side_recv,
    swap_send,
    swap_recv,
):
    me_box, me_dir = lax.axis_index("box"), lax.axis_index("dir")
    z, plane = me_box % RING, me_box // RING
    dx, dy = place_of(z)
    own = TILE * me_box
    slots = ids_hbm.shape[0]
    up, down = (z + 1) % RING, (z + RING - 1) % RING

    here = pl.ds(pl.multiple_of(128 * me_dir, 128), 128)
    loads = [
        pltpu.make_async_copy(src, dst, load_sem.at[at])
        for at, (src, dst) in enumerate(
            (
                (x_hbm, field.at[pl.ds(own, TILE)]),
                (table_hbm, raw.at[pl.ds(0, type_count)]),
                (ids_hbm, ids),
                (types_hbm, types),
                (count_hbm, count),
                (child_hbm, child),
                (octant_hbm, octant),
                (angles_hbm.at[:, here], angles),
                (stencil_hbm.at[:, here], stencil),
                (weights_hbm.at[:, here], weights),
            )
        )
    ]
    for load in loads:
        load.start()

    barrier = pltpu.get_barrier_semaphore()
    for place in (up, down):
        pl.semaphore_signal(
            barrier, inc=1, device_id={"box": RING * plane + place}, device_id_type=MESH
        )
    pl.semaphore_signal(
        barrier, inc=1, device_id={"box": RING * (1 - plane) + z}, device_id_type=MESH
    )
    for step in range(1, 16):
        pl.semaphore_signal(
            barrier, inc=1, device_id={"dir": (me_dir + step) % 16}, device_id_type=MESH
        )
    pl.semaphore_wait(barrier, 18)

    def rows_of(which_plane, origin, start, size):
        return field.at[pl.ds(TILE * (RING * which_plane + origin) + start, size)]

    def hop(way, step, part, origin, first=False):
        here = rows_of(plane, origin, PART * part, PART)
        return pltpu.make_async_remote_copy(
            src_ref=x_hbm.at[pl.ds(PART * part, PART)] if first else here,
            dst_ref=here,
            send_sem=ring_send.at[way, part],
            recv_sem=ring_recv.at[way, step, part],
            device_id={"box": RING * plane + (down if way else up)},
            device_id_type=MESH,
        )

    def side(which_plane, origin, part, shift, size, slot, first=False):
        start = PART * part + shift
        rows = rows_of(which_plane, origin, start, size)
        return pltpu.make_async_remote_copy(
            src_ref=x_hbm.at[pl.ds(start, size)] if first else rows,
            dst_ref=rows,
            send_sem=side_send.at[slot],
            recv_sem=side_recv.at[slot],
            device_id={"box": RING * (1 - plane) + z},
            device_id_type=MESH,
        )

    first_codes = [reach_codes(way, z) for way in range(2)]
    for part, way in ORDER:

        @pl.when(reach_of(first_codes[way], part) > 0)
        def _():
            hop(way, 0, part, z, True).start()

    for part in range(PARTS):
        side(plane, z, part, 0, PART, part, True).start()

    for load in loads:
        load.wait()
    stage_indices(own, type_count, ids, types, count, child, octant, work, stage)
    to_index = pltpu.make_async_copy(stage, index, stage_sem)
    to_index.start()
    build_interp(me_dir, stencil, weights, matrix_high, matrix_low)
    build_phases(angles, phase)
    raw[type_count] = jnp.zeros((2, 128), jnp.float32)
    to_index.wait()

    def fetch(box, carry):
        fetch_operators(slots, box, index, raw, rows)
        return carry

    lax.fori_loop(0, TILE // 2, fetch, 0, unroll=2)

    def ring_step(step, carry):
        origins = [(z + RING - step) % RING, (z + step) % RING]
        codes = [reach_codes(way, origins[way]) for way in range(2)]
        spots = [place_of(origin) for origin in origins]
        for turn, (part, way) in enumerate(ORDER):
            origin, (from_x, from_y) = origins[way], spots[way]
            far = reach_of(codes[way], part)
            half_x, line = part // 2 % 2, part // 4 * 2 + part % 2
            near_y = same_y = from_y == dy
            base = jnp.where(origin // 8 == z // 8, 0, 20)
            if line == 0:
                near_y = near_y | (from_y > dy)
            if line == 3:
                near_y = near_y | (from_y < dy)

            @pl.when(step <= far)
            def _():
                hop(way, step - 1, part, origin).wait_recv()

                @pl.when(step < far)
                def _():
                    hop(way, step, part, origin).start()

                @pl.when(near_y & (from_x == dx))
                def _():
                    slot = base + jnp.where(same_y, part, 8 + half_x)
                    side(plane, origin, part, 0, PART, slot).start()

                @pl.when(near_y & (from_x - dx == 1 - 2 * half_x))
                def _():
                    slot = base + jnp.where(same_y, 10 + 4 * half_x + line, 18 + half_x)
                    side(plane, origin, part, 4 * half_x, 4, slot).start()

            @pl.when(step <= 2)
            def _():
                box = jnp.minimum(16 * (step + 1) + turn, TILE - 1)
                fetch_operators(slots, box, index, raw, rows)

        return carry

    lax.fori_loop(1, HOPS + 1, ring_step, 0)

    def every_side(act, which_plane):
        for half in range(2):
            base = (z // 8 + half) % 2 * 8
            across = base + z_of(dx, 1 - dy)
            for part in range(PARTS):
                act(side(which_plane, base + z % 8, part, 0, PART, 20 * half + part))
            for half_x in range(2):
                slot = 20 * half + 8 + half_x
                act(side(which_plane, across, 5 * dy + 2 * half_x, 0, PART, slot))
            for half_x in range(2):
                to_x = dx + 1 - 2 * half_x

                @pl.when((to_x >= 0) & (to_x <= 3))
                def _():
                    shift = 4 * half_x
                    for line in range(4):
                        part = line // 2 * 4 + line % 2 + 2 * half_x
                        slot = 20 * half + 10 + 4 * half_x + line
                        act(side(which_plane, base + z_of(to_x, dy), part, shift, 4, slot))
                    part, slot = 5 * dy + 2 * half_x, 20 * half + 18 + half_x
                    act(side(which_plane, base + z_of(to_x, 1 - dy), part, shift, 4, slot))

    every_side(lambda copy: copy.wait_recv(), 1 - plane)

    translate_boxes(slots, index, field, rows, moved)
    def swap(to, source):
        return pltpu.make_async_remote_copy(
            src_ref=outbox.at[to],
            dst_ref=inbox.at[source],
            send_sem=swap_send.at[to],
            recv_sem=swap_recv.at[source],
            device_id={"dir": to},
            device_id_type=MESH,
        )

    def pack(step, carry):
        chunk = (me_dir // 4 + 1 + step) % 4
        shift_children(chunk, index, moved, phase, shifted)
        pack_rows(shifted, matrix_high, matrix_low, outbox, chunk)
        for owner in range(4):
            to = 4 * chunk + owner

            @pl.when(to != me_dir)
            def _():
                swap(to, me_dir).start()

        return carry

    lax.fori_loop(0, 4, pack, 0)
    inbox[me_dir] = outbox[me_dir]

    every_side(lambda copy: copy.wait_send(), plane)

    for way in range(2):
        def count(step, sent):
            origin = (z + step) % RING if way else (z + RING - step) % RING
            codes = reach_codes(way, origin)
            return tuple(
                sent[part] + jnp.where(step < reach_of(codes, part), 1, 0) for part in range(PARTS)
            )

        sent = lax.fori_loop(0, HOPS, count, (jnp.int32(0),) * PARTS)
        for part in range(PARTS):
            for total in range(1, HOPS + 1):

                @pl.when(sent[part] == total)
                def _():
                    rows = field.at[pl.ds(0, PART * total)]
                    pltpu.make_async_remote_copy(
                        src_ref=rows,
                        dst_ref=rows,
                        send_sem=ring_send.at[way, part],
                        recv_sem=ring_recv.at[way, 0, part],
                        device_id={"box": RING * plane + (down if way else up)},
                        device_id_type=MESH,
                    ).wait_send()

    def receive(step, carry):
        other = (me_dir + step) % 16
        swap(other, other).wait_recv()
        swap(other, me_dir).wait_send()
        return carry

    lax.fori_loop(1, 16, receive, 0)
    assemble(inbox, out_ref)


def per_device(
    coarse_field,
    trans_table,
    partner_ids,
    partner_types,
    partner_count,
    child_count,
    child_octant,
    dir_angles,
    stencil_ids,
    stencil_weights,
):
    type_count = trans_table.shape[0]
    slots = partner_ids.shape[1]
    f32, i32 = jnp.float32, jnp.int32
    vmem, dma = pltpu.VMEM, pltpu.SemaphoreType.DMA
    return pl.pallas_call(
        functools.partial(kernel, type_count),
        out_shape=jax.ShapeDtypeStruct((16, 2, 4, 512), f32),
        in_specs=[pl.BlockSpec(memory_space=pl.ANY)] * 10,
        out_specs=pl.BlockSpec(memory_space=pltpu.VMEM),
        scratch_shapes=[
            vmem((2048, 8, 128), f32),
            vmem((type_count + 4, 2, 128), f32),
            vmem((TILE, 64, 128), f32),
            vmem((slots, TILE), i32),
            vmem((slots, TILE), i32),
            vmem((1, TILE), i32),
            vmem((1, TILE), i32),
            vmem((2, 128), i32),
            vmem((2, 128), f32),
            vmem((4, 128), i32),
            vmem((4, 128), f32),
            vmem((128, 128), i32),
            vmem((72, 128), i32),
            pltpu.SMEM((72, 128), i32),
            vmem((8, 2, 8, 128), f32),
            vmem((TILE, 2, 8, 128), f32),
            vmem((16, 8, 512), f32),
            vmem((256, 512), jnp.bfloat16),
            vmem((256, 512), jnp.bfloat16),
            vmem((16, 5, 8, 128), f32),
            vmem((16, 5, 8, 128), f32),
            dma((10,)),
            dma,
            dma((2, PARTS)),
            dma((2, HOPS, PARTS)),
            dma((40,)),
            dma((40,)),
            dma((16,)),
            dma((16,)),
        ],
        compiler_params=pltpu.CompilerParams(collective_id=0, has_side_effects=True),
    )(
        coarse_field.reshape(TILE, 8, 128),
        trans_table,
        partner_ids.T,
        partner_types.T,
        partner_count.reshape(1, TILE),
        child_count.reshape(1, TILE),
        child_octant.reshape(2, 128),
        dir_angles,
        stencil_ids.T,
        stencil_weights.T,
    )


def solution(mesh):
    placed = (
        P("box", None, None, "dir"),
        P(None, None, "dir"),
        P("box", None),
        P("box", None),
        P("box"),
        P("box"),
        P("box"),
        P(),
        P(),
        P(),
    )
    return jax.shard_map(
        per_device,
        mesh=mesh,
        in_specs=placed,
        out_specs=P(("box", "dir"), None, None, None),
        check_vma=False,
    )
```

```python
import functools

import jax
import jax.numpy as jnp
from jax import lax
from jax.experimental import pallas as pl
from jax.experimental.pallas import tpu as pltpu
from jax.sharding import PartitionSpec as P

MESH = pl.DeviceIdType.MESH
wave_scale = 3.0

RING = 16
HOPS = 8
TILE = 64
PART = 8
PARTS = 8

REACH = (
    ((8, 0), (8, 0), (1, 8), (1, 8), (8, 0), (2, 8), (1, 8), (3, 8)),
    ((8, 1), (8, 1), (3, 8), (3, 8), (8, 1), (7, 8), (3, 8), (8, 6)),
    ((8, 2), (8, 0), (7, 8), (1, 8), (8, 0), (8, 0), (1, 8), (1, 8)),
    ((8, 3), (8, 1), (6, 8), (3, 8), (8, 1), (8, 1), (3, 8), (3, 8)),
    ((8, 3), (8, 3), (1, 8), (1, 8), (5, 8), (8, 6), (1, 8), (3, 8)),
    ((8, 1), (8, 1), (8, 0), (0, 8), (8, 1), (7, 8), (0, 8), (2, 8)),
    ((6, 8), (8, 3), (8, 7), (1, 8), (8, 3), (8, 3), (1, 8), (1, 8)),
    ((8, 3), (8, 1), (8, 2), (0, 8), (8, 1), (8, 1), (0, 8), (0, 8)),
)

ORDER = (
    (2, 1),
    (4, 1),
    (2, 0),
    (7, 0),
    (6, 1),
    (1, 0),
    (5, 1),
    (3, 0),
    (4, 0),
    (3, 1),
    (1, 1),
    (0, 1),
    (0, 0),
    (7, 1),
    (5, 0),
    (6, 0),
)


def reach_codes(way, origin):
    place = origin % 8
    codes = []
    for base in (0, 4):
        code = jnp.int32(0)
        for which in range(8):
            packed = sum(REACH[which][base + at][way] * 16**at for at in range(4))
            code = jnp.where(place == which, jnp.int32(packed), code)
        codes.append(code)
    return codes


def reach_of(codes, part):
    return codes[part // 4] // 16 ** (part % 4) % 16


def place_of(z):
    return z % 2 + 2 * (z // 4 % 2), z // 2 % 2


def z_of(dx, dy):
    return dx % 2 + 2 * dy + 4 * (dx // 2)


def lane_iota(rows=8):
    return lax.broadcasted_iota(jnp.int32, (rows, 128), 1)


def roll_lanes(value, shift):
    shift = shift % 128
    return pltpu.roll(value, shift, 1) if shift else value


def halves(value):
    high = value.astype(jnp.bfloat16)
    return high, (value - high.astype(jnp.float32)).astype(jnp.bfloat16)


def build_interp(me_dir, ids_ref, weights_ref, high_ref, low_ref):
    relative = (ids_ref[...] - 32 * me_dir + 2 + 512) % 512
    weights = weights_ref[...]
    row = lax.broadcasted_iota(jnp.int32, (128, 128), 0)
    for sub in range(4):
        wanted = (row - 32 * ((sub + me_dir) % 4) + 2 + 128) % 128
        total = jnp.zeros((128, 128), jnp.float32)
        for point in range(4):
            hit = relative[point : point + 1, :] == wanted
            total = total + jnp.where(hit, weights[point : point + 1, :], 0.0)
        inner = (wanted >= 2) & (wanted < 34)
        columns = slice(128 * sub, 128 * sub + 128)
        for at, value in (
            (0, jnp.where(inner, total, 0.0)),
            (128, jnp.where(inner, 0.0, total)),
        ):
            high, low = halves(value)
            high_ref[at : at + 128, columns] = high
            low_ref[at : at + 128, columns] = low


def pack_rows(shifted_ref, high_ref, low_ref, send_ref, chunk):
    high, low = halves(shifted_ref[...].reshape(128, 512))

    def times(left, right):
        return lax.dot_general(
            left, right, (((1,), (1,)), ((), ())), preferred_element_type=jnp.float32
        )

    product = times(high, high_ref[...]) + times(high, low_ref[...]) + times(low, high_ref[...])
    for owner in range(4):
        edges = None
        for line in range(4):
            at = 32 * owner + 8 * line
            send_ref[4 * chunk + owner, line] = product[at : at + 8, 0:128]
            piece = roll_lanes(product[at : at + 8, 128:256], 4 * line)
            edges = piece if edges is None else edges + piece
        send_ref[4 * chunk + owner, 4] = edges


def assemble(got_ref, out_ref):
    lane = lane_iota()
    group = lane // 32
    near = (lane + 2) % 32 < 4
    for sub in range(4):
        moved = (lane - 32 * sub + 128) % 128
        left_from = (moved + 2) // 32 % 4
        right_from = (moved + 96) // 32 % 4
        take_left = moved % 4 >= 2
        for quarter in range(4):
            left = right = None
            for source in range(4):
                left_at = 4 * quarter + source if source else 4 * ((quarter + 1) % 4)
                right_at = 4 * quarter + source if source < 3 else (4 * quarter + 15) % 16
                left_one, right_one = got_ref[left_at, 4], got_ref[right_at, 4]
                left = left_one if left is None else jnp.where(left_from == source, left_one, left)
                right = (
                    right_one if right is None else jnp.where(right_from == source, right_one, right)
                )
            edges = jnp.where(take_left, left, right)
            for line in range(4):
                main = None
                for at in range(4):
                    one = got_ref[4 * quarter + (at - sub) % 4, line]
                    main = one if main is None else jnp.where(group == at, one, main)
                main = roll_lanes(main, -32 * sub)
                extra = roll_lanes(edges, -(32 * sub + 4 * line))
                value = main + jnp.where(near, extra, 0.0)
                columns = slice(128 * quarter, 128 * quarter + 128)
                out_ref[4 * sub + line, 0, :, columns] = value[0:4]
                out_ref[4 * sub + line, 1, :, columns] = value[4:8]


def fetch_operators(slots, box, index_ref, raw_ref, rows_ref):
    for slot in range(slots):
        rows_ref[box, 2 * slot : 2 * slot + 2, :] = raw_ref[index_ref[box, 32 + slot]]


def stage_indices(
    own, type_count, ids_ref, types_ref, count_ref, child_ref, octant_ref, work_ref, stage_ref
):
    slots = ids_ref.shape[0]
    slot = lax.broadcasted_iota(jnp.int32, (slots, TILE), 0)
    box = lax.broadcasted_iota(jnp.int32, (slots, TILE), 1)
    live = slot < count_ref[...]
    work_ref[...] = jnp.zeros((128, 128), jnp.int32)
    source = jnp.where(live, ids_ref[...], own + box)
    work_ref[0:slots, 0:TILE] = source
    work_ref[32 : 32 + slots, 0:TILE] = jnp.where(live, types_ref[...], type_count)
    stage_ref[0:TILE, :] = work_ref[...].T[0:TILE]
    upto = lax.broadcasted_iota(jnp.int32, (TILE, TILE), 0)
    which = lax.broadcasted_iota(jnp.int32, (TILE, TILE), 1)
    bounds = jnp.sum(jnp.where(which <= upto, child_ref[...], 0), axis=1, keepdims=True)
    for half in range(2):
        fine = lax.broadcasted_iota(jnp.int32, (TILE, 128), 1) + 128 * half
        parent = jnp.sum(jnp.where(bounds <= fine, 1, 0), axis=0, keepdims=True)
        parent = jnp.minimum(parent, TILE - 1)
        words = jnp.broadcast_to(parent * 16 + octant_ref[half : half + 1, :], (8, 128))
        at = TILE + 2 * half
        stage_ref[at : at + 1, :] = words[0:1]
        stage_ref[at + 1 : at + 2, :] = pltpu.roll(words, 64, 1)[0:1]


def build_phases(angle_ref, phase_ref):
    theta, phi = angle_ref[0:1, :], angle_ref[1:2, :]
    unit_x = jnp.sin(theta) * jnp.cos(phi)
    unit_y = jnp.sin(theta) * jnp.sin(phi)
    unit_z = jnp.cos(theta)
    octant = lax.broadcasted_iota(jnp.int32, (8, 128), 0)
    sign_x = 1.0 - 2.0 * (octant % 2).astype(jnp.float32)
    sign_y = 1.0 - 2.0 * (octant // 2 % 2).astype(jnp.float32)
    sign_z = 1.0 - 2.0 * (octant // 4).astype(jnp.float32)
    angle = wave_scale * (sign_x * unit_x + sign_y * unit_y + sign_z * unit_z)
    cosine, sine = jnp.cos(angle), jnp.sin(angle)
    for which in range(8):
        phase_ref[which, 0] = jnp.broadcast_to(cosine[which : which + 1], (8, 128))
        spread = jnp.broadcast_to(sine[which : which + 1], (8, 128))
        phase_ref[which, 1] = jnp.where(octant < 4, spread, -spread)


def translate_boxes(slots, index_ref, field_ref, rows_ref, moved_ref):
    real_row = lax.broadcasted_iota(jnp.int32, (8, 128), 0) < 4

    def step(box, carry):
        sums = [None] * 4
        for slot in range(slots):
            source = field_ref[index_ref[box, slot]]
            for part in range(2):
                row = rows_ref[box, 2 * slot + part : 2 * slot + part + 1, :]
                term = jnp.broadcast_to(row, (8, 128)) * source
                at = 2 * (slot % 2) + part
                sums[at] = term if sums[at] is None else sums[at] + term
        straight = sums[0] if sums[2] is None else sums[0] + sums[2]
        crossed = sums[1] if sums[3] is None else sums[1] + sums[3]
        crossed = pltpu.roll(crossed, 4, 0)
        value = straight + jnp.where(real_row, crossed, -crossed)
        moved_ref[box, 0] = value
        moved_ref[box, 1] = pltpu.roll(value, 4, 0)
        return carry

    lax.fori_loop(0, TILE, step, 0, unroll=2)


def shift_children(chunk, index_ref, moved_ref, phase_ref, shifted_ref):
    for owner in range(4):
        for fine in range(16):
            sub, line = fine // 4, fine % 4
            at = 16 * owner + fine
            packed = index_ref[TILE + chunk, at]
            parent, octant = (packed >> 4) & (TILE - 1), packed & 7
            value = (
                moved_ref[parent, 0] * phase_ref[octant, 0]
                + moved_ref[parent, 1] * phase_ref[octant, 1]
            )
            shifted_ref[4 * owner + line, :, 128 * sub : 128 * sub + 128] = value


def kernel(
    type_count,
    x_hbm,
    table_hbm,
    ids_hbm,
    types_hbm,
    count_hbm,
    child_hbm,
    octant_hbm,
    angles_hbm,
    stencil_hbm,
    weights_hbm,
    out_ref,
    field,
    raw,
    rows,
    ids,
    types,
    count,
    child,
    octant,
    angles,
    stencil,
    weights,
    work,
    stage,
    index,
    phase,
    moved,
    shifted,
    matrix_high,
    matrix_low,
    outbox,
    inbox,
    load_sem,
    stage_sem,
    ring_send,
    ring_recv,
    side_send,
    side_recv,
    swap_send,
    swap_recv,
):
    me_box, me_dir = lax.axis_index("box"), lax.axis_index("dir")
    z, plane = me_box % RING, me_box // RING
    dx, dy = place_of(z)
    own = TILE * me_box
    slots = ids_hbm.shape[0]
    up, down = (z + 1) % RING, (z + RING - 1) % RING

    here = pl.ds(pl.multiple_of(128 * me_dir, 128), 128)
    loads = [
        pltpu.make_async_copy(src, dst, load_sem.at[at])
        for at, (src, dst) in enumerate(
            (
                (x_hbm, field.at[pl.ds(own, TILE)]),
                (table_hbm, raw.at[pl.ds(0, type_count)]),
                (ids_hbm, ids),
                (types_hbm, types),
                (count_hbm, count),
                (child_hbm, child),
                (octant_hbm, octant),
                (angles_hbm.at[:, here], angles),
                (stencil_hbm.at[:, here], stencil),
                (weights_hbm.at[:, here], weights),
            )
        )
    ]
    for load in loads:
        load.start()

    barrier = pltpu.get_barrier_semaphore()
    for place in (up, down):
        pl.semaphore_signal(
            barrier, inc=1, device_id={"box": RING * plane + place}, device_id_type=MESH
        )
    pl.semaphore_signal(
        barrier, inc=1, device_id={"box": RING * (1 - plane) + z}, device_id_type=MESH
    )
    for step in range(1, 16):
        pl.semaphore_signal(
            barrier, inc=1, device_id={"dir": (me_dir + step) % 16}, device_id_type=MESH
        )
    pl.semaphore_wait(barrier, 18)

    def rows_of(which_plane, origin, start, size):
        return field.at[pl.ds(TILE * (RING * which_plane + origin) + start, size)]

    def hop(way, step, part, origin, first=False):
        here = rows_of(plane, origin, PART * part, PART)
        return pltpu.make_async_remote_copy(
            src_ref=x_hbm.at[pl.ds(PART * part, PART)] if first else here,
            dst_ref=here,
            send_sem=ring_send.at[way, part],
            recv_sem=ring_recv.at[way, step, part],
            device_id={"box": RING * plane + (down if way else up)},
            device_id_type=MESH,
        )

    def side(which_plane, origin, part, shift, size, slot, first=False):
        start = PART * part + shift
        rows = rows_of(which_plane, origin, start, size)
        return pltpu.make_async_remote_copy(
            src_ref=x_hbm.at[pl.ds(start, size)] if first else rows,
            dst_ref=rows,
            send_sem=side_send.at[slot],
            recv_sem=side_recv.at[slot],
            device_id={"box": RING * (1 - plane) + z},
            device_id_type=MESH,
        )

    first_codes = [reach_codes(way, z) for way in range(2)]
    for part, way in ORDER:

        @pl.when(reach_of(first_codes[way], part) > 0)
        def _():
            hop(way, 0, part, z, True).start()

    for part in range(PARTS):
        side(plane, z, part, 0, PART, part, True).start()

    for load in loads:
        load.wait()
    stage_indices(own, type_count, ids, types, count, child, octant, work, stage)
    to_index = pltpu.make_async_copy(stage, index, stage_sem)
    to_index.start()
    build_interp(me_dir, stencil, weights, matrix_high, matrix_low)
    build_phases(angles, phase)
    raw[type_count] = jnp.zeros((2, 128), jnp.float32)
    to_index.wait()

    def fetch(box, carry):
        fetch_operators(slots, box, index, raw, rows)
        return carry

    lax.fori_loop(0, TILE, fetch, 0, unroll=2)

    def ring_step(step, carry):
        origins = [(z + RING - step) % RING, (z + step) % RING]
        codes = [reach_codes(way, origins[way]) for way in range(2)]
        spots = [place_of(origin) for origin in origins]
        for part, way in ORDER:
            origin, (from_x, from_y) = origins[way], spots[way]
            far = reach_of(codes[way], part)
            half_x, line = part // 2 % 2, part // 4 * 2 + part % 2
            near_y = same_y = from_y == dy
            base = jnp.where(origin // 8 == z // 8, 0, 20)
            if line == 0:
                near_y = near_y | (from_y > dy)
            if line == 3:
                near_y = near_y | (from_y < dy)

            @pl.when(step <= far)
            def _():
                hop(way, step - 1, part, origin).wait_recv()

                @pl.when(step < far)
                def _():
                    hop(way, step, part, origin).start()

                @pl.when(near_y & (from_x == dx))
                def _():
                    slot = base + jnp.where(same_y, part, 8 + half_x)
                    side(plane, origin, part, 0, PART, slot).start()

                @pl.when(near_y & (from_x - dx == 1 - 2 * half_x))
                def _():
                    slot = base + jnp.where(same_y, 10 + 4 * half_x + line, 18 + half_x)
                    side(plane, origin, part, 4 * half_x, 4, slot).start()

        return carry

    lax.fori_loop(1, HOPS + 1, ring_step, 0)

    def every_side(act, which_plane):
        for half in range(2):
            base = (z // 8 + half) % 2 * 8
            across = base + z_of(dx, 1 - dy)
            for part in range(PARTS):
                act(side(which_plane, base + z % 8, part, 0, PART, 20 * half + part))
            for half_x in range(2):
                slot = 20 * half + 8 + half_x
                act(side(which_plane, across, 5 * dy + 2 * half_x, 0, PART, slot))
            for half_x in range(2):
                to_x = dx + 1 - 2 * half_x

                @pl.when((to_x >= 0) & (to_x <= 3))
                def _():
                    shift = 4 * half_x
                    for line in range(4):
                        part = line // 2 * 4 + line % 2 + 2 * half_x
                        slot = 20 * half + 10 + 4 * half_x + line
                        act(side(which_plane, base + z_of(to_x, dy), part, shift, 4, slot))
                    part, slot = 5 * dy + 2 * half_x, 20 * half + 18 + half_x
                    act(side(which_plane, base + z_of(to_x, 1 - dy), part, shift, 4, slot))

    every_side(lambda copy: copy.wait_recv(), 1 - plane)

    translate_boxes(slots, index, field, rows, moved)
    def swap(to, source):
        return pltpu.make_async_remote_copy(
            src_ref=outbox.at[to],
            dst_ref=inbox.at[source],
            send_sem=swap_send.at[to],
            recv_sem=swap_recv.at[source],
            device_id={"dir": to},
            device_id_type=MESH,
        )

    def pack(step, carry):
        chunk = (me_dir // 4 + 1 + step) % 4
        shift_children(chunk, index, moved, phase, shifted)
        pack_rows(shifted, matrix_high, matrix_low, outbox, chunk)
        for owner in range(4):
            to = 4 * chunk + owner

            @pl.when(to != me_dir)
            def _():
                swap(to, me_dir).start()

        return carry

    lax.fori_loop(0, 4, pack, 0)
    inbox[me_dir] = outbox[me_dir]

    every_side(lambda copy: copy.wait_send(), plane)

    for way in range(2):
        def count(step, sent):
            origin = (z + step) % RING if way else (z + RING - step) % RING
            codes = reach_codes(way, origin)
            return tuple(
                sent[part] + jnp.where(step < reach_of(codes, part), 1, 0) for part in range(PARTS)
            )

        sent = lax.fori_loop(0, HOPS, count, (jnp.int32(0),) * PARTS)
        for part in range(PARTS):
            for total in range(1, HOPS + 1):

                @pl.when(sent[part] == total)
                def _():
                    rows = field.at[pl.ds(0, PART * total)]
                    pltpu.make_async_remote_copy(
                        src_ref=rows,
                        dst_ref=rows,
                        send_sem=ring_send.at[way, part],
                        recv_sem=ring_recv.at[way, 0, part],
                        device_id={"box": RING * plane + (down if way else up)},
                        device_id_type=MESH,
                    ).wait_send()

    def receive(step, carry):
        other = (me_dir + step) % 16
        swap(other, other).wait_recv()
        swap(other, me_dir).wait_send()
        return carry

    lax.fori_loop(1, 16, receive, 0)
    assemble(inbox, out_ref)


def per_device(
    coarse_field,
    trans_table,
    partner_ids,
    partner_types,
    partner_count,
    child_count,
    child_octant,
    dir_angles,
    stencil_ids,
    stencil_weights,
):
    type_count = trans_table.shape[0]
    slots = partner_ids.shape[1]
    f32, i32 = jnp.float32, jnp.int32
    vmem, dma = pltpu.VMEM, pltpu.SemaphoreType.DMA
    return pl.pallas_call(
        functools.partial(kernel, type_count),
        out_shape=jax.ShapeDtypeStruct((16, 2, 4, 512), f32),
        in_specs=[pl.BlockSpec(memory_space=pl.ANY)] * 10,
        out_specs=pl.BlockSpec(memory_space=pltpu.VMEM),
        scratch_shapes=[
            vmem((2048, 8, 128), f32),
            vmem((type_count + 4, 2, 128), f32),
            vmem((TILE, 64, 128), f32),
            vmem((slots, TILE), i32),
            vmem((slots, TILE), i32),
            vmem((1, TILE), i32),
            vmem((1, TILE), i32),
            vmem((2, 128), i32),
            vmem((2, 128), f32),
            vmem((4, 128), i32),
            vmem((4, 128), f32),
            vmem((128, 128), i32),
            vmem((72, 128), i32),
            pltpu.SMEM((72, 128), i32),
            vmem((8, 2, 8, 128), f32),
            vmem((TILE, 2, 8, 128), f32),
            vmem((16, 8, 512), f32),
            vmem((256, 512), jnp.bfloat16),
            vmem((256, 512), jnp.bfloat16),
            vmem((16, 5, 8, 128), f32),
            vmem((16, 5, 8, 128), f32),
            dma((10,)),
            dma,
            dma((2, PARTS)),
            dma((2, HOPS, PARTS)),
            dma((40,)),
            dma((40,)),
            dma((16,)),
            dma((16,)),
        ],
        compiler_params=pltpu.CompilerParams(collective_id=0, has_side_effects=True),
    )(
        coarse_field.reshape(TILE, 8, 128),
        trans_table,
        partner_ids.T,
        partner_types.T,
        partner_count.reshape(1, TILE),
        child_count.reshape(1, TILE),
        child_octant.reshape(2, 128),
        dir_angles,
        stencil_ids.T,
        stencil_weights.T,
    )


def solution(mesh):
    placed = (
        P("box", None, None, "dir"),
        P(None, None, "dir"),
        P("box", None),
        P("box", None),
        P("box"),
        P("box"),
        P("box"),
        P(),
        P(),
        P(),
    )
    return jax.shard_map(
        per_device,
        mesh=mesh,
        in_specs=placed,
        out_specs=P(("box", "dir"), None, None, None),
        check_vma=False,
    )
```
